32 devices in a mesh: pipe: 2 (over y), tensor: 4 (over z), dp: 4 (over x, core).
Axes of the slice: x: 2, y: 2, z: 4, core: 2. Of those that a mesh axis runs over, the one named last changes fastest.
Arguments:
- weights: bfloat16 [2, 4096, 4096], P('pipe', None, 'tensor'), may hold values from -0.09375 to 0.09375
- codes: int32 [2, 1024, 4096], P('pipe', 'dp'), may hold values from -127 to 127
- scales: float32 [2, 1024], P('pipe', 'dp'), may hold values from 0.004 to 0.04
- grad_out: bfloat16 [1024, 4096], P('dp', 'tensor'), may hold values from -6 to 6
Outputs:
- grad_in: bfloat16 [2, 1024, 4096], P('pipe', 'dp', 'tensor')
- weight_grad: float32 [2, 4096, 4096], P('pipe', 'dp', 'tensor')
The draws below stay inside these ranges and needn't reach their ends.
Inputs may be any that keep to these rules, and one draw needn't show every extreme that they name: Symmetric integer codes of a per-token quantization.
All inputs are finite; a program needn't handle non-finite values.
Results may differ from the reference program's by a relative error of at most 0.028.
Values may be sent and summed in bfloat16 or wider, within the bound.
A program may use at most 64 MiB of HBM per device.

```python
import math
import jax
import jax.numpy as jnp
from jax import lax

D = 4096
TOK_DEV = 256
TOKENS = 1024
SECTIONS = 2
COLS = 1024
N_TENSOR = 4
N_DP = 4


def with_ends(result, key, low, largest):
    extent = result.shape
    index_at = [jax.random.randint(jax.random.fold_in(key, axis), (), 0, extent[axis]) for axis in range(len(extent))]
    result = result.at[tuple(index_at)].set(low)
    longest = extent.index(max(extent))
    index_at[longest] = (index_at[longest] + 1) % extent[longest]
    return result.at[tuple(index_at)].set(largest)


def levels(own_key, dims, split, least, top_value):
    factor_of = 1.0
    for position, shards_of in split:
        steps = jax.random.uniform(jax.random.fold_in(jax.random.fold_in(own_key, 6), position), (shards_of,), jnp.float32, least / len(split), top_value / len(split))
        factor_of = factor_of * jnp.repeat(jnp.exp(steps), dims[position] // shards_of).reshape((-1,) + (1,) * (len(dims) - 1 - position))
    return factor_of


def centred(stream_key, shape, deviation, most, cuts=(), held_as=jnp.bfloat16):
    gain = levels(stream_key, shape, cuts, -0.22, 0.18) if cuts else 1.0
    drawn = jax.random.normal(stream_key, shape, jnp.float32) * deviation * gain
    return jnp.minimum(jnp.maximum(drawn, -most), most).astype(held_as)


def setup_inputs(seed: int = 0) -> dict:
    key_of = jax.random.split(jax.random.key(seed), 5)
    weights = centred(key_of[0], (SECTIONS, D, D), D ** -0.5, 0.09375, ((0, 2), (2, 4)))
    codes = with_ends(jax.random.randint(key_of[1], (SECTIONS, TOKENS, D), -127, 128), jax.random.fold_in(key_of[1], 1), -127, 127).astype(jnp.int32)
    scales = jnp.clip(jnp.exp(math.log(0.04) - 2.30258502 * jax.random.uniform(key_of[2], (SECTIONS, TOKENS), jnp.float32) ** levels(key_of[2], (SECTIONS, TOKENS), ((0, 2), (1, 4)), -0.2, 0.2)), 0.004, 0.04)
    grad_out = centred(key_of[3], (TOKENS, D), 1.0, 6.0, ((0, 4), (1, 4)))
    return dict(weights=weights, codes=codes, scales=scales, grad_out=grad_out)


def reference(weights, codes, scales, grad_out):
    arriving = grad_out
    grad_list = []
    weight_list = []
    for section_index in range(SECTIONS - 1, -1, -1):
        section_weight = weights[section_index]

        def add_block(running, block_index):
            grad_block = lax.dynamic_slice_in_dim(arriving, block_index * COLS, COLS, 1)
            weight_block = lax.dynamic_slice_in_dim(section_weight, block_index * COLS, COLS, 1)
            block_term = lax.dot_general(grad_block, weight_block, (((1,), (1,)), ((), ())), preferred_element_type=jnp.float32).astype(jnp.bfloat16)
            block_term = lax.optimization_barrier(block_term)
            return running + block_term.astype(jnp.float32), None

        summed, _ = lax.scan(add_block, arriving.astype(jnp.float32), jnp.arange(N_TENSOR, dtype=jnp.int32))
        fresh_grad = summed.astype(jnp.bfloat16)
        dequant = (codes[section_index].astype(jnp.float32) * scales[section_index][:, None]).astype(jnp.bfloat16)
        section_arriving = arriving

        def add_group(running, group_index):
            start = group_index * TOK_DEV
            x_group = lax.dynamic_slice_in_dim(dequant, start, TOK_DEV, 0)
            g_group = lax.dynamic_slice_in_dim(section_arriving, start, TOK_DEV, 0)
            group_term = lax.dot_general(x_group, g_group, (((0,), (0,)), ((), ())), preferred_element_type=jnp.float32).astype(jnp.bfloat16)
            group_term = lax.optimization_barrier(group_term)
            return running + group_term.astype(jnp.float32), None

        weight_term, _ = lax.scan(add_group, jnp.zeros((D, D), jnp.float32), jnp.arange(N_DP, dtype=jnp.int32))
        grad_list.insert(0, fresh_grad)
        weight_list.insert(0, weight_term)
        arriving = fresh_grad
    return jnp.stack(grad_list), jnp.stack(weight_list)
```

```python
import functools

import jax
import jax.numpy as jnp
from jax import lax
from jax.experimental import pallas as pl
from jax.experimental.pallas import tpu as pltpu
from jax.sharding import PartitionSpec as P

MICRO = 8
FAR_LAG, MID_LAG, END_LAG, PASS_LAG = 1, 3, 4, 4
LATE = 2
CODES_AT = 1
PROMPT, WAIT = 1, 1
NT = (((1,), (1,)), ((), ()))
TN = (((0,), (0,)), ((), ()))


def relay_kernel(
    weights, codes, scales, grad_out,
    grad_in, weight_grad,
    w_buf, c_buf, r_buf, s_buf, x_buf, x_all, g_all, prod, from_left, from_right, from_end,
    w_sem, c_sem, s_sem, g_sem, hop_send, hop_recv,
    sum_send, sum_recv, end_send, end_recv,
    g_send, g_recv, pass_send, pass_recv, x_send, x_recv,
    *, sections, shards, replicas,
):
    section, shard, replica = (lax.axis_index(n) for n in ("pipe", "tensor", "dp"))
    is_last = section == sections - 1
    tok, cols = grad_in.shape
    width = x_buf.shape[2]
    rows = tok // MICRO
    pairs = replicas // 2
    pair, side = replica // 2, lax.rem(replica, 2)
    sibling = 2 * pair + 1 - side
    at_left, at_right = shard == 0, shard == shards - 1
    at_end = at_left | at_right

    barrier = pltpu.get_barrier_semaphore()

    def greet(condition, target):
        @pl.when(condition)
        def _():
            pl.semaphore_signal(barrier, inc=1, device_id=target)

    def w_copy(j):
        part = pl.ds(pl.multiple_of(j * cols, cols), cols)
        return pltpu.make_async_copy(weights.at[part, :], w_buf.at[part, :], w_sem.at[j])

    def c_copy(o):
        peer = lax.rem(replica + o, replicas)
        part = pl.ds(pl.multiple_of(peer * width, width), width)
        return pltpu.make_async_copy(codes.at[:, part], c_buf.at[o], c_sem.at[o])

    def s_copy():
        return pltpu.make_async_copy(scales, r_buf, s_sem)

    def strip(m):
        return pl.ds(pl.multiple_of(m * rows, rows), rows)

    def held(source, m):
        return pl.ds(pl.multiple_of(source * tok + m * rows, rows), rows)

    def block(source):
        return pl.ds(pl.multiple_of(source * tok, tok), tok)

    def g_load():
        return pltpu.make_async_copy(grad_out, g_all.at[block(replica), :], g_sem)

    def order(i):
        step = jnp.where(at_end & (i < 2), 1 - i, i)
        return jnp.where(2 * shard < shards, shards - 1 - step, step)

    def load_codes():
        s_copy().start()

        @pl.loop(0, replicas)
        def _(i):
            c_copy(replicas - 1 - i).start()

    @pl.when(is_last)
    def _():
        g_load().start()

    @pl.when(jnp.logical_not(is_last))
    def _():
        load_codes()

    @pl.loop(0, shards)
    def _(i):
        w_copy(order(i)).start()

    greet(shard > 0, {"tensor": shard - 1})
    greet(shard < shards - 1, {"tensor": shard + 1})
    greet(at_end, {"tensor": shards - 1 - shard})
    greet(section > 0, {"pipe": section - 1})
    greet(section < sections - 1, {"pipe": section + 1})

    @pl.loop(1, replicas)
    def _(o):
        pl.semaphore_signal(barrier, inc=1, device_id={"dp": lax.rem(replica + o, replicas)})

    def one(condition):
        return jnp.where(condition, 1, 0)

    pl.semaphore_wait(
        barrier,
        replicas - 1 + one(shard > 0) + one(shard < shards - 1) + one(at_end) + one(section > 0) + one(section < sections - 1),
    )

    def hop(m):
        return pltpu.make_async_remote_copy(
            src_ref=grad_in.at[strip(m), :], dst_ref=g_all.at[held(replica, m), :],
            send_sem=hop_send, recv_sem=hop_recv.at[m], device_id={"pipe": section - 1})

    def to_right(m, j):
        return pltpu.make_async_remote_copy(
            src_ref=prod.at[j, strip(m), :], dst_ref=from_left.at[j, strip(m), :],
            send_sem=sum_send.at[j], recv_sem=sum_recv.at[m, j + 1], device_id={"tensor": shard + 1})

    def to_left(m, j):
        return pltpu.make_async_remote_copy(
            src_ref=prod.at[j, strip(m), :], dst_ref=from_right.at[j, strip(m), :],
            send_sem=sum_send.at[j], recv_sem=sum_recv.at[m, j], device_id={"tensor": shard - 1})

    def to_end(m):
        j = shards - 1 - shard
        return pltpu.make_async_remote_copy(
            src_ref=prod.at[j, strip(m), :], dst_ref=from_end.at[strip(m), :],
            send_sem=end_send, recv_sem=end_recv.at[m], device_id={"tensor": j})

    def g_share(m):
        return pltpu.make_async_remote_copy(
            src_ref=g_all.at[held(replica, m), :], dst_ref=g_all.at[held(replica, m), :],
            send_sem=g_send.at[0], recv_sem=g_recv.at[m, 0], device_id={"dp": sibling})

    def g_cross(m, o):
        return pltpu.make_async_remote_copy(
            src_ref=g_all.at[held(replica, m), :], dst_ref=g_all.at[held(replica, m), :],
            send_sem=g_send.at[o], recv_sem=g_recv.at[m, o],
            device_id={"dp": 2 * lax.rem(pair + o, pairs) + side})

    def g_pass(m, o):
        source = 2 * lax.rem(pair + pairs - o, pairs) + side
        return pltpu.make_async_remote_copy(
            src_ref=g_all.at[held(source, m), :], dst_ref=g_all.at[held(source, m), :],
            send_sem=pass_send.at[o], recv_sem=pass_recv.at[m, o], device_id={"dp": sibling})

    def x_share(o):
        return pltpu.make_async_remote_copy(
            src_ref=x_buf.at[o], dst_ref=x_all.at[block(replica), :],
            send_sem=x_send.at[o], recv_sem=x_recv.at[o],
            device_id={"dp": lax.rem(replica + o, replicas)})

    def dequantize():
        s_copy().wait()
        s_buf[...] = jnp.transpose(jnp.broadcast_to(r_buf[...], (128, tok)))

        @pl.loop(0, replicas)
        def _(i):
            o = replicas - 1 - i
            c_copy(o).wait()

            @pl.loop(0, 4)
            def _(m):
                part = pl.ds(pl.multiple_of(m * (tok // 4), tok // 4), tok // 4)
                own = pl.ds(pl.multiple_of(replica * tok + m * (tok // 4), tok // 4), tok // 4)
                value = (c_buf[o, part, :].astype(jnp.float32) * s_buf[part, 0:1]).astype(jnp.bfloat16)

                @pl.when(o > 0)
                def _():
                    x_buf[o, part, :] = value

                @pl.when(o == 0)
                def _():
                    x_all[own, :] = value

            @pl.when(o > 0)
            def _():
                x_share(o).start()

    def launch(m, j):
        straight = j == shards - 1 - shard

        @pl.when(at_end & straight)
        def _():
            to_end(m).start()

        @pl.when(at_left & (j > 0) & jnp.logical_not(straight))
        def _():
            to_right(m, j).start()

        @pl.when(at_right & (j < shards - 1) & jnp.logical_not(straight))
        def _():
            to_left(m, j).start()

    def launch_next(m):
        @pl.when(shard == 1)
        def _():
            to_right(m, shards - 1).start()

        @pl.when(shard == shards - 2)
        def _():
            to_left(m, 0).start()

    def spread(m):
        g_share(m).start()

        @pl.loop(1, pairs)
        def _(o):
            g_cross(m, o).start()

    def pass_on(m):
        @pl.loop(1, pairs)
        def _(o):
            g_cross(m, o).wait_recv()
            g_pass(m, o).start()

    def w_part(j):
        return w_buf[pl.ds(pl.multiple_of(j * cols, cols), cols), :]

    def produce_all():
        g_load().wait()

        @pl.loop(0, shards)
        def _(i):
            j = order(i)
            w_copy(j).wait()
            prod[j, :, :] = lax.dot_general(
                g_all[block(replica), :], w_part(j), NT, preferred_element_type=jnp.float32
            ).astype(jnp.bfloat16)
            launch(0, j)

            @pl.when(i == 0)
            def _():
                launch_next(0)

        @pl.loop(1, MICRO)
        def _(m):
            @pl.loop(0, shards)
            def _(i):
                launch(m, order(i))

        load_codes()

        @pl.loop(0, MICRO)
        def _(m):
            spread(m)

    def produce(m):
        hop(m).wait_recv()
        spread(m)

        @pl.loop(0, shards)
        def _(i):
            j = order(i)
            prod[j, strip(m), :] = lax.dot_general(
                g_all[held(replica, m), :], w_part(j), NT, preferred_element_type=jnp.float32
            ).astype(jnp.bfloat16)
            launch(m, j)

            @pl.when(i == 0)
            def _():
                launch_next(m)

    def add_in(m, j, arrived):
        part = strip(m)
        total = prod[j, part, :].astype(jnp.float32) + arrived[j, part, :].astype(jnp.float32)
        prod[j, part, :] = total.astype(jnp.bfloat16)

    def relay(m, rightward):
        @pl.loop(0, shards - 1)
        def _(i):
            far = shards - 1 - i
            right, left = shard + far, shard - far

            @pl.when(rightward & (shard > 0) & (right < shards) & ((shard > 1) | (right < shards - 1)))
            def _():
                to_right(m, right).wait_recv()
                add_in(m, right, from_left)
                to_right(m, right).start()

            @pl.when(jnp.logical_not(rightward) & (shard < shards - 1) & (left >= 0) & ((shard < shards - 2) | (left > 0)))
            def _():
                to_left(m, left).wait_recv()
                add_in(m, left, from_right)
                to_left(m, left).start()

    def finish(m):
        part = strip(m)

        @pl.when(shard > 0)
        def _():
            to_right(m, shard).wait_recv()

        @pl.when(shard < shards - 1)
        def _():
            to_left(m, shard).wait_recv()

        @pl.when(at_end)
        def _():
            to_end(m).wait_recv()

        def of(ref):
            return ref[shard, part, :].astype(jnp.float32)

        own = of(prod) + g_all[held(replica, m), :].astype(jnp.float32)

        @pl.when(jnp.logical_not(at_end))
        def _():
            grad_in[part, :] = (own + (of(from_left) + of(from_right))).astype(jnp.bfloat16)

        def settle(condition, inner):
            @pl.when(condition)
            def _():
                grad_in[part, :] = (own + (of(inner) + from_end[part, :].astype(jnp.float32))).astype(jnp.bfloat16)

        settle(at_left, from_right)
        settle(at_right, from_left)

        @pl.when(section > 0)
        def _():
            hop(m).start()

    near = 2 * shard < shards

    def relays(m):
        relay(m, near)
        relay(m, jnp.logical_not(near))

    @pl.when(is_last)
    def _():
        produce_all()

        @pl.loop(0, MICRO)
        def _(m):
            @pl.when(m + 1 < MICRO)
            def _():
                launch_next(m + 1)

            @pl.when(at_end)
            def _():
                finish(m)

            @pl.when(jnp.logical_not(at_end))
            def _():
                relays(m)

                @pl.when(m < PROMPT)
                def _():
                    finish(m)

                @pl.when(m >= PROMPT + WAIT)
                def _():
                    finish(m - WAIT)

            @pl.when(m == CODES_AT)
            def _():
                dequantize()

        @pl.when(jnp.logical_not(at_end))
        def _():
            @pl.loop(MICRO - WAIT, MICRO)
            def _(m):
                finish(m)

        @pl.loop(0, MICRO)
        def _(m):
            pass_on(m)

    @pl.when(jnp.logical_not(is_last))
    def _():
        dequantize()

        @pl.loop(0, shards)
        def _(i):
            w_copy(order(i)).wait()

        behind = jnp.where(at_end, END_LAG, MID_LAG)

        @pl.loop(0, MICRO)
        def _(s):
            def at(lag, action):
                @pl.when(s >= lag)
                def _():
                    action(s - lag)

            produce(s)
            at(FAR_LAG, lambda m: relay(m, jnp.logical_not(near)))
            at(PASS_LAG, pass_on)
            at(behind, finish)
            relay(s, near)

        @pl.loop(MICRO - FAR_LAG, MICRO)
        def _(m):
            relay(m, jnp.logical_not(near))

        @pl.loop(MICRO - PASS_LAG, MICRO)
        def _(m):
            pass_on(m)

        @pl.loop(MICRO - behind, MICRO - LATE)
        def _(m):
            finish(m)

    @pl.loop(1, replicas)
    def _(o):
        x_share(o).wait_recv()

    @pl.loop(0, MICRO)
    def _(m):
        g_share(m).wait_recv()

        @pl.loop(1, pairs)
        def _(o):
            g_pass(m, o).wait_recv()

    chunk = min(width, 256)

    @pl.loop(0, width // chunk)
    def _(i):
        part = pl.ds(pl.multiple_of(i * chunk, chunk), chunk)
        weight_grad[part, :] = lax.dot_general(x_all[:, part], g_all[...], TN, preferred_element_type=jnp.float32)

    @pl.when(jnp.logical_not(is_last))
    def _():
        @pl.loop(MICRO - LATE, MICRO)
        def _(m):
            finish(m)

    def sent(source, sem):
        pltpu.make_async_copy(source, source, sem).wait()

    @pl.loop(0, shards)
    def _(j):
        @pl.when((j != shard) & jnp.logical_not(at_end & (j == shards - 1 - shard)))
        def _():
            sent(prod.at[j], sum_send.at[j])

    @pl.when(at_end)
    def _():
        sent(prod.at[shards - 1 - shard], end_send)

    @pl.when(section > 0)
    def _():
        sent(grad_in, hop_send)

    sent(g_all.at[block(replica), :], g_send.at[0])

    @pl.loop(1, pairs)
    def _(o):
        sent(g_all.at[block(replica), :], g_send.at[o])
        sent(g_all.at[block(replica), :], pass_send.at[o])

    @pl.loop(1, replicas)
    def _(o):
        x_share(o).wait_send()


def per_device(weights, codes, scales, grad_out):
    sections, shards, replicas = (lax.axis_size(n) for n in ("pipe", "tensor", "dp"))
    tok, cols = grad_out.shape
    depth = weights.shape[1]
    width = depth // replicas
    pairs = replicas // 2
    low = jnp.bfloat16
    dma = pltpu.SemaphoreType.DMA
    far = pl.BlockSpec(memory_space=pltpu.MemorySpace.HBM)
    inside = pl.BlockSpec(memory_space=pltpu.VMEM)
    grad_in, weight_grad = pl.pallas_call(
        functools.partial(relay_kernel, sections=sections, shards=shards, replicas=replicas),
        out_shape=(
            pltpu.VMEM((tok, cols), low),
            pltpu.VMEM((width, cols), jnp.float32),
        ),
        in_specs=[far, far, far, far],
        out_specs=(inside, inside),
        scratch_shapes=[
            pltpu.VMEM((depth, cols), low),
            pltpu.VMEM((replicas, tok, width), jnp.int32),
            pltpu.VMEM((1, tok), jnp.float32),
            pltpu.VMEM((tok, 128), jnp.float32),
            pltpu.VMEM((replicas, tok, width), low),
            pltpu.VMEM((replicas * tok, width), low),
            pltpu.VMEM((replicas * tok, cols), low),
            pltpu.VMEM((shards, tok, cols), low),
            pltpu.VMEM((shards, tok, cols), low),
            pltpu.VMEM((shards, tok, cols), low),
            pltpu.VMEM((tok, cols), low),
            dma((shards,)), dma((replicas,)), dma(()), dma(()), dma(()), dma((MICRO,)),
            dma((shards,)), dma((MICRO, shards + 1)), dma(()), dma((MICRO,)),
            dma((pairs,)), dma((MICRO, pairs)), dma((pairs,)), dma((MICRO, pairs)),
            dma((replicas,)), dma((replicas,)),
        ],
        compiler_params=pltpu.CompilerParams(collective_id=0, has_side_effects=True, vmem_limit_bytes=58 * 2**20),
    )(weights[0], codes[0], scales, grad_out)
    return grad_in[None], weight_grad[None]


def solution(mesh):
    placed = (P("pipe", None, "tensor"), P("pipe", "dp", None), P("pipe", "dp"), P("dp", "tensor"))
    return jax.shard_map(
        per_device,
        mesh=mesh,
        in_specs=placed,
        out_specs=(P("pipe", "dp", "tensor"), P("pipe", "dp", "tensor")),
        check_vma=False,
    )
```

```python
import functools

import jax
import jax.numpy as jnp
from jax import lax
from jax.experimental import pallas as pl
from jax.experimental.pallas import tpu as pltpu
from jax.sharding import PartitionSpec as P

MICRO = 8
FAR_LAG, MID_LAG, END_LAG, PASS_LAG = 1, 3, 4, 4
LATE = 2
CODES_AT = 1
PROMPT, WAIT = 1, 1
FILL, FULL = 2, 6
DRAIN, STOP = 4, 8
LEAD = 2
NT = (((1,), (1,)), ((), ()))
TN = (((0,), (0,)), ((), ()))


def relay_kernel(
    weights, codes, scales, grad_out,
    grad_in, weight_grad,
    w_buf, c_buf, r_buf, s_buf, x_buf, x_all, g_all, prod, from_left, from_right, from_end, stage,
    w_sem, c_sem, s_sem, g_sem, hop_send, hop_recv,
    sum_send, sum_recv, end_send, end_recv, stage_recv, carry_send,
    g_send, g_recv, pass_send, pass_recv, x_send, x_recv,
    *, sections, shards, replicas,
):
    section, shard, replica = (lax.axis_index(n) for n in ("pipe", "tensor", "dp"))
    is_last = section == sections - 1
    tok, cols = grad_in.shape
    width = x_buf.shape[2]
    rows = tok // MICRO
    pairs = replicas // 2
    pair, side = replica // 2, lax.rem(replica, 2)
    sibling = 2 * pair + 1 - side
    at_left, at_right = shard == 0, shard == shards - 1
    at_end = at_left | at_right

    barrier = pltpu.get_barrier_semaphore()

    def greet(condition, target):
        @pl.when(condition)
        def _():
            pl.semaphore_signal(barrier, inc=1, device_id=target)

    def w_copy(j):
        part = pl.ds(pl.multiple_of(j * cols, cols), cols)
        return pltpu.make_async_copy(weights.at[part, :], w_buf.at[part, :], w_sem.at[j])

    def c_copy(o):
        peer = lax.rem(replica + o, replicas)
        part = pl.ds(pl.multiple_of(peer * width, width), width)
        return pltpu.make_async_copy(codes.at[:, part], c_buf.at[o], c_sem.at[o])

    def s_copy():
        return pltpu.make_async_copy(scales, r_buf, s_sem)

    def strip(m):
        return pl.ds(pl.multiple_of(m * rows, rows), rows)

    def held(source, m):
        return pl.ds(pl.multiple_of(source * tok + m * rows, rows), rows)

    def block(source):
        return pl.ds(pl.multiple_of(source * tok, tok), tok)

    def g_load():
        return pltpu.make_async_copy(grad_out, g_all.at[block(replica), :], g_sem)

    def order(i):
        step = jnp.where(at_end & (i < 2), 1 - i, i)
        return jnp.where(2 * shard < shards, shards - 1 - step, step)

    def load_codes():
        s_copy().start()

        @pl.loop(0, replicas)
        def _(i):
            c_copy(replicas - 1 - i).start()

    @pl.when(is_last)
    def _():
        g_load().start()

    @pl.when(jnp.logical_not(is_last))
    def _():
        load_codes()

    @pl.loop(0, shards)
    def _(i):
        w_copy(order(i)).start()

    greet(shard > 0, {"tensor": shard - 1})
    greet(shard < shards - 1, {"tensor": shard + 1})
    greet(at_end, {"tensor": shards - 1 - shard})
    greet(at_end & (section > 0), {"pipe": section - 1, "tensor": shards - 1 - shard})
    greet(at_end & (section < sections - 1), {"pipe": section + 1, "tensor": shards - 1 - shard})
    greet(section > 0, {"pipe": section - 1})
    greet(section < sections - 1, {"pipe": section + 1})

    @pl.loop(1, replicas)
    def _(o):
        pl.semaphore_signal(barrier, inc=1, device_id={"dp": lax.rem(replica + o, replicas)})

    def one(condition):
        return jnp.where(condition, 1, 0)

    pl.semaphore_wait(
        barrier,
        replicas - 1 + one(shard > 0) + one(shard < shards - 1) + one(at_end) + one(section > 0)
        + one(section < sections - 1) + one(at_end & (section > 0)) + one(at_end & (section < sections - 1)),
    )

    def hop(m):
        return pltpu.make_async_remote_copy(
            src_ref=grad_in.at[strip(m), :], dst_ref=g_all.at[held(replica, m), :],
            send_sem=hop_send, recv_sem=hop_recv.at[m], device_id={"pipe": section - 1})

    def to_right(m, j):
        return pltpu.make_async_remote_copy(
            src_ref=prod.at[j, strip(m), :], dst_ref=from_left.at[j, strip(m), :],
            send_sem=sum_send.at[j], recv_sem=sum_recv.at[m, j + 1], device_id={"tensor": shard + 1})

    def to_left(m, j):
        return pltpu.make_async_remote_copy(
            src_ref=prod.at[j, strip(m), :], dst_ref=from_right.at[j, strip(m), :],
            send_sem=sum_send.at[j], recv_sem=sum_recv.at[m, j], device_id={"tensor": shard - 1})

    def to_end(m):
        j = shards - 1 - shard
        return pltpu.make_async_remote_copy(
            src_ref=prod.at[j, strip(m), :], dst_ref=from_end.at[strip(m), :],
            send_sem=end_send, recv_sem=end_recv.at[m], device_id={"tensor": j})

    def detoured(m):
        return jnp.where(is_last, (m >= FILL) & (m < FULL), (m >= DRAIN) & (m < STOP))

    def to_stage(m, k):
        return pltpu.make_async_remote_copy(
            src_ref=prod.at[shards - 1 - shard, strip(m), :], dst_ref=stage.at[k, strip(m), :],
            send_sem=end_send, recv_sem=stage_recv.at[k, m], device_id={"pipe": section + (2 * k - 1)})

    def carry(m, k):
        to_stage(m, k).wait_recv()
        pltpu.make_async_remote_copy(
            src_ref=stage.at[k, strip(m), :], dst_ref=from_end.at[strip(m), :],
            send_sem=carry_send.at[k], recv_sem=end_recv.at[m],
            device_id={"pipe": section + (1 - 2 * k), "tensor": shards - 1 - shard}).start()

    def carry_all(start, stop, k):
        @pl.loop(start, stop)
        def _(m):
            carry(m, k)

    def g_share(m):
        return pltpu.make_async_remote_copy(
            src_ref=g_all.at[held(replica, m), :], dst_ref=g_all.at[held(replica, m), :],
            send_sem=g_send.at[0], recv_sem=g_recv.at[m, 0], device_id={"dp": sibling})

    def g_cross(m, o):
        return pltpu.make_async_remote_copy(
            src_ref=g_all.at[held(replica, m), :], dst_ref=g_all.at[held(replica, m), :],
            send_sem=g_send.at[o], recv_sem=g_recv.at[m, o],
            device_id={"dp": 2 * lax.rem(pair + o, pairs) + side})

    def g_pass(m, o):
        source = 2 * lax.rem(pair + pairs - o, pairs) + side
        return pltpu.make_async_remote_copy(
            src_ref=g_all.at[held(source, m), :], dst_ref=g_all.at[held(source, m), :],
            send_sem=pass_send.at[o], recv_sem=pass_recv.at[m, o], device_id={"dp": sibling})

    def x_share(o):
        return pltpu.make_async_remote_copy(
            src_ref=x_buf.at[o], dst_ref=x_all.at[block(replica), :],
            send_sem=x_send.at[o], recv_sem=x_recv.at[o],
            device_id={"dp": lax.rem(replica + o, replicas)})

    def dequantize():
        s_copy().wait()
        s_buf[...] = jnp.transpose(jnp.broadcast_to(r_buf[...], (128, tok)))

        @pl.loop(0, replicas)
        def _(i):
            o = replicas - 1 - i
            c_copy(o).wait()

            @pl.loop(0, 4)
            def _(m):
                part = pl.ds(pl.multiple_of(m * (tok // 4), tok // 4), tok // 4)
                own = pl.ds(pl.multiple_of(replica * tok + m * (tok // 4), tok // 4), tok // 4)
                value = (c_buf[o, part, :].astype(jnp.float32) * s_buf[part, 0:1]).astype(jnp.bfloat16)

                @pl.when(o > 0)
                def _():
                    x_buf[o, part, :] = value

                @pl.when(o == 0)
                def _():
                    x_all[own, :] = value

            @pl.when(o > 0)
            def _():
                x_share(o).start()

    def launch(m, j):
        straight = j == shards - 1 - shard

        @pl.when(at_end & straight & jnp.logical_not(detoured(m)))
        def _():
            to_end(m).start()

        @pl.when(at_end & straight & detoured(m) & is_last)
        def _():
            to_stage(m, 0).start()

        @pl.when(at_end & straight & detoured(m) & jnp.logical_not(is_last))
        def _():
            to_stage(m, 1).start()

        @pl.when(at_left & (j > 0) & jnp.logical_not(straight))
        def _():
            to_right(m, j).start()

        @pl.when(at_right & (j < shards - 1) & jnp.logical_not(straight))
        def _():
            to_left(m, j).start()

    def launch_next(m):
        @pl.when(shard == 1)
        def _():
            to_right(m, shards - 1).start()

        @pl.when(shard == shards - 2)
        def _():
            to_left(m, 0).start()

    def spread(m):
        g_share(m).start()

        @pl.loop(1, pairs)
        def _(o):
            g_cross(m, o).start()

    def pass_on(m):
        @pl.loop(1, pairs)
        def _(o):
            g_cross(m, o).wait_recv()
            g_pass(m, o).start()

    def w_part(j):
        return w_buf[pl.ds(pl.multiple_of(j * cols, cols), cols), :]

    def produce_all():
        g_load().wait()

        @pl.loop(0, shards)
        def _(i):
            j = order(i)
            w_copy(j).wait()
            prod[j, :, :] = lax.dot_general(
                g_all[block(replica), :], w_part(j), NT, preferred_element_type=jnp.float32
            ).astype(jnp.bfloat16)
            launch(0, j)

            @pl.when(i == 0)
            def _():
                @pl.loop(0, LEAD)
                def _(m):
                    launch_next(m)

        @pl.loop(1, MICRO)
        def _(m):
            @pl.loop(0, shards)
            def _(i):
                launch(m, order(i))

        load_codes()

        @pl.loop(0, MICRO)
        def _(m):
            spread(m)

    def produce(m):
        hop(m).wait_recv()
        spread(m)

        @pl.loop(0, shards)
        def _(i):
            j = order(i)
            prod[j, strip(m), :] = lax.dot_general(
                g_all[held(replica, m), :], w_part(j), NT, preferred_element_type=jnp.float32
            ).astype(jnp.bfloat16)
            launch(m, j)

            @pl.when(i == 0)
            def _():
                launch_next(m)

    def add_in(m, j, arrived):
        part = strip(m)
        total = prod[j, part, :].astype(jnp.float32) + arrived[j, part, :].astype(jnp.float32)
        prod[j, part, :] = total.astype(jnp.bfloat16)

    def relay(m, rightward):
        @pl.loop(0, shards - 1)
        def _(i):
            far = shards - 1 - i
            right, left = shard + far, shard - far

            @pl.when(rightward & (shard > 0) & (right < shards) & ((shard > 1) | (right < shards - 1)))
            def _():
                to_right(m, right).wait_recv()
                add_in(m, right, from_left)
                to_right(m, right).start()

            @pl.when(jnp.logical_not(rightward) & (shard < shards - 1) & (left >= 0) & ((shard < shards - 2) | (left > 0)))
            def _():
                to_left(m, left).wait_recv()
                add_in(m, left, from_right)
                to_left(m, left).start()

    def finish(m):
        part = strip(m)

        @pl.when(shard > 0)
        def _():
            to_right(m, shard).wait_recv()

        @pl.when(shard < shards - 1)
        def _():
            to_left(m, shard).wait_recv()

        @pl.when(at_end)
        def _():
            to_end(m).wait_recv()

        def of(ref):
            return ref[shard, part, :].astype(jnp.float32)

        own = of(prod) + g_all[held(replica, m), :].astype(jnp.float32)

        @pl.when(jnp.logical_not(at_end))
        def _():
            grad_in[part, :] = (own + (of(from_left) + of(from_right))).astype(jnp.bfloat16)

        def settle(condition, inner):
            @pl.when(condition)
            def _():
                grad_in[part, :] = (own + (of(inner) + from_end[part, :].astype(jnp.float32))).astype(jnp.bfloat16)

        settle(at_left, from_right)
        settle(at_right, from_left)

        @pl.when(section > 0)
        def _():
            hop(m).start()

    near = 2 * shard < shards

    def relays(m):
        relay(m, near)
        relay(m, jnp.logical_not(near))

    @pl.when(is_last)
    def _():
        produce_all()

        @pl.loop(0, MICRO)
        def _(m):
            @pl.when(at_end)
            def _():
                finish(m)

            @pl.when(jnp.logical_not(at_end))
            def _():
                relays(m)

                @pl.when(m + LEAD < MICRO)
                def _():
                    launch_next(m + LEAD)

                @pl.when(m < PROMPT)
                def _():
                    finish(m)

                @pl.when(m >= PROMPT + WAIT)
                def _():
                    finish(m - WAIT)

            @pl.when(m == CODES_AT)
            def _():
                dequantize()

        @pl.when(jnp.logical_not(at_end))
        def _():
            @pl.loop(MICRO - WAIT, MICRO)
            def _(m):
                finish(m)

        @pl.loop(0, MICRO)
        def _(m):
            pass_on(m)

    below, above = at_end & (section > 0), at_end & (section == sections - 2)

    @pl.when(jnp.logical_not(is_last))
    def _():
        dequantize()

        @pl.when(above)
        def _():
            carry_all(FILL, FULL, 0)

        @pl.loop(0, shards)
        def _(i):
            w_copy(order(i)).wait()

        behind = jnp.where(at_end, END_LAG, MID_LAG)

        @pl.loop(0, MICRO)
        def _(s):
            def at(lag, action):
                @pl.when(s >= lag)
                def _():
                    action(s - lag)

            produce(s)
            at(FAR_LAG, lambda m: relay(m, jnp.logical_not(near)))
            at(PASS_LAG, pass_on)
            at(behind, finish)
            relay(s, near)

        @pl.loop(MICRO - FAR_LAG, MICRO)
        def _(m):
            relay(m, jnp.logical_not(near))

        @pl.loop(MICRO - PASS_LAG, MICRO)
        def _(m):
            pass_on(m)

        @pl.loop(MICRO - behind, MICRO - LATE)
        def _(m):
            finish(m)

    @pl.when(below)
    def _():
        carry_all(DRAIN, STOP, 1)

    @pl.loop(1, replicas)
    def _(o):
        x_share(o).wait_recv()

    @pl.loop(0, MICRO)
    def _(m):
        g_share(m).wait_recv()

        @pl.loop(1, pairs)
        def _(o):
            g_pass(m, o).wait_recv()

    chunk = min(width, 256)

    @pl.loop(0, width // chunk)
    def _(i):
        part = pl.ds(pl.multiple_of(i * chunk, chunk), chunk)
        weight_grad[part, :] = lax.dot_general(x_all[:, part], g_all[...], TN, preferred_element_type=jnp.float32)

    @pl.when(jnp.logical_not(is_last))
    def _():
        @pl.loop(MICRO - LATE, MICRO)
        def _(m):
            finish(m)

    def sent(source, sem):
        pltpu.make_async_copy(source, source, sem).wait()

    @pl.loop(0, shards)
    def _(j):
        @pl.when((j != shard) & jnp.logical_not(at_end & (j == shards - 1 - shard)))
        def _():
            sent(prod.at[j], sum_send.at[j])

    @pl.when(at_end)
    def _():
        sent(prod.at[shards - 1 - shard], end_send)

    @pl.when(above)
    def _():
        sent(stage.at[0, pl.ds(0, (FULL - FILL) * rows), :], carry_send.at[0])

    @pl.when(below)
    def _():
        sent(stage.at[1, pl.ds(0, (STOP - DRAIN) * rows), :], carry_send.at[1])

    @pl.when(section > 0)
    def _():
        sent(grad_in, hop_send)

    sent(g_all.at[block(replica), :], g_send.at[0])

    @pl.loop(1, pairs)
    def _(o):
        sent(g_all.at[block(replica), :], g_send.at[o])
        sent(g_all.at[block(replica), :], pass_send.at[o])

    @pl.loop(1, replicas)
    def _(o):
        x_share(o).wait_send()


def per_device(weights, codes, scales, grad_out):
    sections, shards, replicas = (lax.axis_size(n) for n in ("pipe", "tensor", "dp"))
    tok, cols = grad_out.shape
    depth = weights.shape[1]
    width = depth // replicas
    pairs = replicas // 2
    low = jnp.bfloat16
    dma = pltpu.SemaphoreType.DMA
    far = pl.BlockSpec(memory_space=pltpu.MemorySpace.HBM)
    inside = pl.BlockSpec(memory_space=pltpu.VMEM)
    grad_in, weight_grad = pl.pallas_call(
        functools.partial(relay_kernel, sections=sections, shards=shards, replicas=replicas),
        out_shape=(
            pltpu.VMEM((tok, cols), low),
            pltpu.VMEM((width, cols), jnp.float32),
        ),
        in_specs=[far, far, far, far],
        out_specs=(inside, inside),
        scratch_shapes=[
            pltpu.VMEM((depth, cols), low),
            pltpu.VMEM((replicas, tok, width), jnp.int32),
            pltpu.VMEM((1, tok), jnp.float32),
            pltpu.VMEM((tok, 128), jnp.float32),
            pltpu.VMEM((replicas, tok, width), low),
            pltpu.VMEM((replicas * tok, width), low),
            pltpu.VMEM((replicas * tok, cols), low),
            pltpu.VMEM((shards, tok, cols), low),
            pltpu.VMEM((shards, tok, cols), low),
            pltpu.VMEM((shards, tok, cols), low),
            pltpu.VMEM((tok, cols), low),
            pltpu.VMEM((2, tok, cols), low),
            dma((shards,)), dma((replicas,)), dma(()), dma(()), dma(()), dma((MICRO,)),
            dma((shards,)), dma((MICRO, shards + 1)), dma(()), dma((MICRO,)), dma((2, MICRO)), dma((2,)),
            dma((pairs,)), dma((MICRO, pairs)), dma((pairs,)), dma((MICRO, pairs)),
            dma((replicas,)), dma((replicas,)),
        ],
        compiler_params=pltpu.CompilerParams(collective_id=0, has_side_effects=True, vmem_limit_bytes=58 * 2**20),
    )(weights[0], codes[0], scales, grad_out)
    return grad_in[None], weight_grad[None]


def solution(mesh):
    placed = (P("pipe", None, "tensor"), P("pipe", "dp", None), P("pipe", "dp"), P("dp", "tensor"))
    return jax.shard_map(
        per_device,
        mesh=mesh,
        in_specs=placed,
        out_specs=(P("pipe", "dp", "tensor"), P("pipe", "dp", "tensor")),
        check_vma=False,
    )
```

```python
import functools

import jax
import jax.numpy as jnp
from jax import lax
from jax.experimental import pallas as pl
from jax.experimental.pallas import tpu as pltpu
from jax.sharding import PartitionSpec as P

MICRO = 8
NEAR_LAG, FAR_LAG, MID_LAG, END_LAG, PASS_LAG = 1, 1, 3, 4, 4
MID_LATE, END_LATE = 3, 4
CODES_AT = 1
PROMPT, WAIT = 1, 1
FILL, FULL = 1, 5
DRAIN, STOP = 4, 8
LEAD = 2
STEPS, KEPT = 4, 2
LIMIT = 32
NT = (((1,), (1,)), ((), ()))
TN = (((0,), (0,)), ((), ()))


def rows_a_step(width):
    return max(width // STEPS, 128)


def closing_kernel(grad, part, x_all, g_all, grad_in, weight_grad, held, sems, own_sem, part_sem):
    done, width = part.shape[0], x_all.shape[1]
    chunk = rows_a_step(width)
    copies = [
        pltpu.make_async_copy(part, weight_grad.at[pl.ds(0, done), :], part_sem),
        pltpu.make_async_copy(grad, grad_in, own_sem),
    ]
    for copy in copies:
        copy.start()
    for i, start in enumerate(range(done, width, chunk)):
        held[i, :, :] = lax.dot_general(
            x_all[:, pl.ds(start, chunk)], g_all[...], TN, preferred_element_type=jnp.float32)
        copies.append(pltpu.make_async_copy(held.at[i], weight_grad.at[pl.ds(start, chunk), :], sems.at[i]))
        copies[-1].start()
    for copy in copies:
        copy.wait()


def relay_kernel(
    weights, codes, scales, grad_out,
    grad_in, weight_part, x_all, g_all,
    w_buf, c_buf, r_buf, s_buf, x_buf, prod, from_left, from_right, from_end, stage,
    w_sem, c_sem, s_sem, g_sem, hop_send, hop_recv,
    sum_send, sum_recv, end_send, end_recv, stage_recv, carry_send,
    g_send, share_recv, g_recv, pass_send, pass_recv, x_send, x_recv,
    *, sections, shards, replicas,
):
    section, shard, replica = (lax.axis_index(n) for n in ("pipe", "tensor", "dp"))
    is_last = section == sections - 1
    tok, cols = grad_in.shape
    width = x_buf.shape[2]
    rows = tok // MICRO
    pairs = replicas // 2
    pair, side = replica // 2, lax.rem(replica, 2)
    sibling = 2 * pair + 1 - side
    at_left, at_right = shard == 0, shard == shards - 1
    at_end = at_left | at_right

    barrier = pltpu.get_barrier_semaphore()

    def greet(condition, target):
        @pl.when(condition)
        def _():
            pl.semaphore_signal(barrier, inc=1, device_id=target)

    def w_copy(j):
        part = pl.ds(pl.multiple_of(j * cols, cols), cols)
        return pltpu.make_async_copy(weights.at[part, :], w_buf.at[part, :], w_sem.at[j])

    def c_copy(o):
        peer = lax.rem(replica + o, replicas)
        part = pl.ds(pl.multiple_of(peer * width, width), width)
        return pltpu.make_async_copy(codes.at[:, part], c_buf.at[o], c_sem.at[o])

    def s_copy():
        return pltpu.make_async_copy(scales, r_buf, s_sem)

    def strip(m):
        return pl.ds(pl.multiple_of(m * rows, rows), rows)

    def held(source, m):
        return pl.ds(pl.multiple_of(source * tok + m * rows, rows), rows)

    def block(source):
        return pl.ds(pl.multiple_of(source * tok, tok), tok)

    def g_load():
        return pltpu.make_async_copy(grad_out, g_all.at[block(replica), :], g_sem)

    def order(i):
        step = jnp.where(at_end & (i < 2), 1 - i, i)
        return jnp.where(2 * shard < shards, shards - 1 - step, step)

    def load_codes():
        s_copy().start()

        @pl.loop(0, replicas)
        def _(i):
            c_copy(replicas - 1 - i).start()

    @pl.when(is_last)
    def _():
        g_load().start()

    @pl.when(jnp.logical_not(is_last))
    def _():
        load_codes()

    @pl.loop(0, shards)
    def _(i):
        w_copy(order(i)).start()

    greet(shard > 0, {"tensor": shard - 1})
    greet(shard < shards - 1, {"tensor": shard + 1})
    greet(at_end, {"tensor": shards - 1 - shard})
    greet(section > 0, {"pipe": section - 1})
    greet(section < sections - 1, {"pipe": section + 1})

    @pl.loop(1, replicas)
    def _(o):
        pl.semaphore_signal(barrier, inc=1, device_id={"dp": lax.rem(replica + o, replicas)})

    def one(condition):
        return jnp.where(condition, 1, 0)

    pl.semaphore_wait(
        barrier,
        replicas - 1 + one(shard > 0) + one(shard < shards - 1) + one(at_end) + one(section > 0)
        + one(section < sections - 1),
    )

    def hop(m):
        return pltpu.make_async_remote_copy(
            src_ref=grad_in.at[strip(m), :], dst_ref=g_all.at[held(replica, m), :],
            send_sem=hop_send, recv_sem=hop_recv.at[m], device_id={"pipe": section - 1})

    def to_right(m, j):
        return pltpu.make_async_remote_copy(
            src_ref=prod.at[j, strip(m), :], dst_ref=from_left.at[j, strip(m), :],
            send_sem=sum_send.at[j], recv_sem=sum_recv.at[m, j + 1], device_id={"tensor": shard + 1})

    def to_left(m, j):
        return pltpu.make_async_remote_copy(
            src_ref=prod.at[j, strip(m), :], dst_ref=from_right.at[j, strip(m), :],
            send_sem=sum_send.at[j], recv_sem=sum_recv.at[m, j], device_id={"tensor": shard - 1})

    def to_end(m):
        j = shards - 1 - shard
        return pltpu.make_async_remote_copy(
            src_ref=prod.at[j, strip(m), :], dst_ref=from_end.at[strip(m), :],
            send_sem=end_send, recv_sem=end_recv.at[m], device_id={"tensor": j})

    def detoured(m):
        return jnp.where(is_last, (m >= FILL) & (m < FULL), (m >= DRAIN) & (m < STOP))

    def to_stage(m, k):
        return pltpu.make_async_remote_copy(
            src_ref=prod.at[shards - 1 - shard, strip(m), :], dst_ref=stage.at[k, strip(m), :],
            send_sem=end_send, recv_sem=stage_recv.at[k, m - (FILL, DRAIN)[k]], device_id={"pipe": section + (2 * k - 1)})

    def carry(m, k):
        to_stage(m, k).wait_recv()
        pltpu.make_async_remote_copy(
            src_ref=stage.at[k, strip(m), :], dst_ref=from_end.at[strip(m), :],
            send_sem=carry_send.at[k], recv_sem=end_recv.at[m],
            device_id={"pipe": section + (1 - 2 * k), "tensor": shards - 1 - shard}).start()

    def carry_all(start, stop, k):
        @pl.loop(start, stop)
        def _(m):
            carry(m, k)

    def g_share(m):
        return pltpu.make_async_remote_copy(
            src_ref=g_all.at[held(replica, m), :], dst_ref=g_all.at[held(replica, m), :],
            send_sem=g_send.at[0], recv_sem=share_recv, device_id={"dp": sibling})

    def g_cross(m, o):
        return pltpu.make_async_remote_copy(
            src_ref=g_all.at[held(replica, m), :], dst_ref=g_all.at[held(replica, m), :],
            send_sem=g_send.at[o], recv_sem=g_recv.at[m, o - 1],
            device_id={"dp": 2 * lax.rem(pair + o, pairs) + side})

    def g_pass(m, o):
        source = 2 * lax.rem(pair + pairs - o, pairs) + side
        return pltpu.make_async_remote_copy(
            src_ref=g_all.at[held(source, m), :], dst_ref=g_all.at[held(source, m), :],
            send_sem=pass_send.at[o], recv_sem=pass_recv.at[o], device_id={"dp": sibling})

    def x_share(o):
        return pltpu.make_async_remote_copy(
            src_ref=x_buf.at[o], dst_ref=x_all.at[block(replica), :],
            send_sem=x_send.at[o], recv_sem=x_recv.at[o],
            device_id={"dp": lax.rem(replica + o, replicas)})

    def dequantize():
        s_copy().wait()
        s_buf[...] = jnp.transpose(jnp.broadcast_to(r_buf[...], (128, tok)))

        @pl.loop(0, replicas)
        def _(i):
            o = replicas - 1 - i
            c_copy(o).wait()

            @pl.loop(0, 4)
            def _(m):
                part = pl.ds(pl.multiple_of(m * (tok // 4), tok // 4), tok // 4)
                own = pl.ds(pl.multiple_of(replica * tok + m * (tok // 4), tok // 4), tok // 4)
                value = (c_buf[o, part, :].astype(jnp.float32) * s_buf[part, 0:1]).astype(jnp.bfloat16)

                @pl.when(o > 0)
                def _():
                    x_buf[o, part, :] = value

                @pl.when(o == 0)
                def _():
                    x_all[own, :] = value

            @pl.when(o > 0)
            def _():
                x_share(o).start()

    def launch(m, j):
        straight = j == shards - 1 - shard

        @pl.when(at_end & straight & jnp.logical_not(detoured(m)))
        def _():
            to_end(m).start()

        @pl.when(at_end & straight & detoured(m) & is_last)
        def _():
            to_stage(m, 0).start()

        @pl.when(at_end & straight & detoured(m) & jnp.logical_not(is_last))
        def _():
            to_stage(m, 1).start()

        @pl.when(at_left & (j > 0) & jnp.logical_not(straight))
        def _():
            to_right(m, j).start()

        @pl.when(at_right & (j < shards - 1) & jnp.logical_not(straight))
        def _():
            to_left(m, j).start()

    def launch_next(m):
        @pl.when(shard == 1)
        def _():
            to_right(m, shards - 1).start()

        @pl.when(shard == shards - 2)
        def _():
            to_left(m, 0).start()

    def spread(m):
        g_share(m).start()

        @pl.loop(1, pairs)
        def _(o):
            g_cross(m, o).start()

    def pass_on(m):
        @pl.loop(1, pairs)
        def _(o):
            g_cross(m, o).wait_recv()
            g_pass(m, o).start()

    def w_part(j):
        return w_buf[pl.ds(pl.multiple_of(j * cols, cols), cols), :]

    def produce_all():
        g_load().wait()

        @pl.loop(0, shards)
        def _(i):
            j = order(i)
            w_copy(j).wait()
            prod[j, :, :] = lax.dot_general(
                g_all[block(replica), :], w_part(j), NT, preferred_element_type=jnp.float32
            ).astype(jnp.bfloat16)
            launch(0, j)

            @pl.when(i == 0)
            def _():
                @pl.loop(0, LEAD)
                def _(m):
                    launch_next(m)

        @pl.when(at_end)
        def _():
            @pl.loop(1, MICRO)
            def _(m):
                @pl.loop(0, shards)
                def _(i):
                    launch(m, order(i))

    def produce(m):
        hop(m).wait_recv()
        spread(m)

        @pl.loop(0, shards)
        def _(i):
            j = order(i)
            prod[j, strip(m), :] = lax.dot_general(
                g_all[held(replica, m), :], w_part(j), NT, preferred_element_type=jnp.float32
            ).astype(jnp.bfloat16)
            launch(m, j)

            @pl.when(i == 0)
            def _():
                launch_next(m)

    def add_in(m, j, arrived):
        part = strip(m)
        total = prod[j, part, :].astype(jnp.float32) + arrived[j, part, :].astype(jnp.float32)
        prod[j, part, :] = total.astype(jnp.bfloat16)

    def relay(m, rightward):
        @pl.loop(0, shards - 1)
        def _(i):
            far = shards - 1 - i
            right, left = shard + far, shard - far

            @pl.when(rightward & (shard > 0) & (right < shards) & ((shard > 1) | (right < shards - 1)))
            def _():
                to_right(m, right).wait_recv()
                add_in(m, right, from_left)
                to_right(m, right).start()

            @pl.when(jnp.logical_not(rightward) & (shard < shards - 1) & (left >= 0) & ((shard < shards - 2) | (left > 0)))
            def _():
                to_left(m, left).wait_recv()
                add_in(m, left, from_right)
                to_left(m, left).start()

    def finish(m):
        part = strip(m)

        @pl.when(shard > 0)
        def _():
            to_right(m, shard).wait_recv()

        @pl.when(shard < shards - 1)
        def _():
            to_left(m, shard).wait_recv()

        @pl.when(at_end)
        def _():
            to_end(m).wait_recv()

        def of(ref):
            return ref[shard, part, :].astype(jnp.float32)

        own = of(prod) + g_all[held(replica, m), :].astype(jnp.float32)

        @pl.when(jnp.logical_not(at_end))
        def _():
            grad_in[part, :] = (own + (of(from_left) + of(from_right))).astype(jnp.bfloat16)

        def settle(condition, inner):
            @pl.when(condition)
            def _():
                grad_in[part, :] = (own + (of(inner) + from_end[part, :].astype(jnp.float32))).astype(jnp.bfloat16)

        settle(at_left, from_right)
        settle(at_right, from_left)

        @pl.when(section > 0)
        def _():
            hop(m).start()

    near = 2 * shard < shards
    late = jnp.where(at_end, END_LATE, MID_LATE)

    def relays(m):
        relay(m, near)
        relay(m, jnp.logical_not(near))

    @pl.when(is_last)
    def _():
        produce_all()

        @pl.loop(0, MICRO)
        def _(m):
            @pl.when(jnp.logical_not(at_end))
            def _():
                relays(m)

                @pl.when(m + LEAD < MICRO)
                def _():
                    launch_next(m + LEAD)

            @pl.when(m == 0)
            def _():
                load_codes()

                @pl.loop(0, MICRO)
                def _(n):
                    spread(n)

            @pl.when(at_end)
            def _():
                finish(m)

            @pl.when(jnp.logical_not(at_end))
            def _():
                @pl.when(m < PROMPT)
                def _():
                    finish(m)

                @pl.when(m >= PROMPT + WAIT)
                def _():
                    finish(m - WAIT)

            @pl.when(m == CODES_AT)
            def _():
                dequantize()

        @pl.when(jnp.logical_not(at_end))
        def _():
            @pl.loop(MICRO - WAIT, MICRO)
            def _(m):
                finish(m)

        @pl.loop(0, MICRO)
        def _(m):
            pass_on(m)

    below, above = at_end & (section > 0), at_end & (section == sections - 2)

    @pl.when(jnp.logical_not(is_last))
    def _():
        dequantize()

        @pl.when(above)
        def _():
            carry_all(FILL, FULL, 0)

        @pl.loop(0, shards)
        def _(i):
            w_copy(order(i)).wait()

        behind = jnp.where(at_end, END_LAG, MID_LAG)

        @pl.loop(0, MICRO)
        def _(s):
            def at(lag, action):
                @pl.when(s >= lag)
                def _():
                    action(s - lag)

            produce(s)
            at(NEAR_LAG, lambda m: relay(m, near))
            at(FAR_LAG, lambda m: relay(m, jnp.logical_not(near)))
            at(PASS_LAG, pass_on)
            at(behind, finish)

        @pl.loop(MICRO - NEAR_LAG, MICRO)
        def _(m):
            relay(m, near)

        @pl.loop(MICRO - FAR_LAG, MICRO)
        def _(m):
            relay(m, jnp.logical_not(near))

        @pl.loop(MICRO - PASS_LAG, MICRO)
        def _(m):
            pass_on(m)

        @pl.loop(MICRO - behind, MICRO - late)
        def _(m):
            finish(m)

    @pl.when(below)
    def _():
        carry_all(DRAIN, STOP, 1)

    @pl.loop(1, replicas)
    def _(o):
        x_share(o).wait_recv()

    def sent(source, sem):
        pltpu.make_async_copy(source, source, sem).wait()

    sent(g_all.at[block(sibling), :], share_recv)

    @pl.loop(1, pairs)
    def _(o):
        sent(g_all.at[block(2 * lax.rem(pair + pairs - o, pairs) + 1 - side), :], pass_recv.at[o])

    chunk = rows_a_step(width)

    @pl.loop(0, weight_part.shape[0] // chunk)
    def _(i):
        part = pl.ds(pl.multiple_of(i * chunk, chunk), chunk)
        weight_part[part, :] = lax.dot_general(x_all[:, part], g_all[...], TN, preferred_element_type=jnp.float32)

    @pl.when(jnp.logical_not(is_last))
    def _():
        @pl.loop(MICRO - late, MICRO)
        def _(m):
            finish(m)

    @pl.loop(0, shards)
    def _(j):
        @pl.when((j != shard) & jnp.logical_not(at_end & (j == shards - 1 - shard)))
        def _():
            sent(prod.at[j], sum_send.at[j])

    @pl.when(at_end)
    def _():
        sent(prod.at[shards - 1 - shard], end_send)

    @pl.when(above)
    def _():
        sent(stage.at[0, pl.ds(0, (FULL - FILL) * rows), :], carry_send.at[0])

    @pl.when(below)
    def _():
        sent(stage.at[1, pl.ds(0, (STOP - DRAIN) * rows), :], carry_send.at[1])

    @pl.when(section > 0)
    def _():
        sent(grad_in, hop_send)

    sent(g_all.at[block(replica), :], g_send.at[0])

    @pl.loop(1, pairs)
    def _(o):
        sent(g_all.at[block(replica), :], g_send.at[o])
        sent(g_all.at[block(replica), :], pass_send.at[o])

    @pl.loop(1, replicas)
    def _(o):
        x_share(o).wait_send()


def per_device(weights, codes, scales, grad_out):
    sections, shards, replicas = (lax.axis_size(n) for n in ("pipe", "tensor", "dp"))
    tok, cols = grad_out.shape
    depth = weights.shape[1]
    width = depth // replicas
    pairs = replicas // 2
    low = jnp.bfloat16
    dma = pltpu.SemaphoreType.DMA
    far = pl.BlockSpec(memory_space=pltpu.MemorySpace.HBM)
    inside = pl.BlockSpec(memory_space=pltpu.VMEM)
    chunk = rows_a_step(width)
    done = min(KEPT, width // chunk - 1) * chunk
    later = (width - done) // chunk
    handed = pl.pallas_call(
        functools.partial(relay_kernel, sections=sections, shards=shards, replicas=replicas),
        out_shape=(
            pltpu.VMEM((tok, cols), low),
            pltpu.VMEM((done, cols), jnp.float32),
            pltpu.VMEM((replicas * tok, width), low),
            pltpu.VMEM((replicas * tok, cols), low),
        ),
        in_specs=[far, far, far, far],
        out_specs=(inside,) * 4,
        scratch_shapes=[
            pltpu.VMEM((depth, cols), low),
            pltpu.VMEM((replicas, tok, width), jnp.int32),
            pltpu.VMEM((1, tok), jnp.float32),
            pltpu.VMEM((tok, 128), jnp.float32),
            pltpu.VMEM((replicas, tok, width), low),
            pltpu.VMEM((shards, tok, cols), low),
            pltpu.VMEM((shards, tok, cols), low),
            pltpu.VMEM((shards, tok, cols), low),
            pltpu.VMEM((tok, cols), low),
            pltpu.VMEM((2, tok, cols), low),
            dma((shards,)), dma((replicas,)), dma(()), dma(()), dma(()), dma((MICRO,)),
            dma((shards,)), dma((MICRO, shards + 1)), dma(()), dma((MICRO,)), dma((2, max(FULL - FILL, STOP - DRAIN))), dma((2,)),
            dma((pairs,)), dma(()), dma((MICRO, pairs - 1)), dma((pairs,)), dma((pairs,)),
            dma((replicas,)), dma((replicas,)),
        ],
        compiler_params=pltpu.CompilerParams(collective_id=0, has_side_effects=True, vmem_limit_bytes=57 * 2**20),
    )(weights[0], codes[0], scales, grad_out)
    grad_in, weight_grad = pl.pallas_call(
        closing_kernel,
        out_shape=(
            jax.ShapeDtypeStruct((tok, cols), low),
            jax.ShapeDtypeStruct((width, cols), jnp.float32),
        ),
        in_specs=[inside] * 4,
        out_specs=(far, far),
        scratch_shapes=[pltpu.VMEM((later, chunk, cols), jnp.float32), dma((later,)), dma(()), dma(())],
        compiler_params=pltpu.CompilerParams(vmem_limit_bytes=LIMIT * 2**20),
    )(*handed)
    return grad_in[None], weight_grad[None]


def solution(mesh):
    placed = (P("pipe", None, "tensor"), P("pipe", "dp", None), P("pipe", "dp"), P("dp", "tensor"))
    return jax.shard_map(
        per_device,
        mesh=mesh,
        in_specs=placed,
        out_specs=(P("pipe", "dp", "tensor"), P("pipe", "dp", "tensor")),
        check_vma=False,
    )
```

```python
import functools

import jax
import jax.numpy as jnp
from jax import lax
from jax.experimental import pallas as pl
from jax.experimental.pallas import tpu as pltpu
from jax.sharding import PartitionSpec as P

MICRO = 8
NEAR_LAG, FAR_LAG, MID_LAG, END_LAG, PASS_LAG = 1, 1, 3, 4, 4
MID_LATE, END_LATE = 3, 4
CODES_AT = 1
PROMPT, WAIT = 1, 1
FILL, FULL = 1, 5
DRAIN, STOP = 4, 8
LEAD = 2
STEPS, KEPT = 4, 2
LIMIT = 32
NT = (((1,), (1,)), ((), ()))
TN = (((0,), (0,)), ((), ()))


def rows_a_step(width):
    return max(width // STEPS, 128)


def closing_kernel(grad, part, x_all, g_all, grad_in, weight_grad, held, sems, own_sem, part_sem):
    done, width = part.shape[0], x_all.shape[1]
    chunk = rows_a_step(width)
    copies = [
        pltpu.make_async_copy(part, weight_grad.at[pl.ds(0, done), :], part_sem),
        pltpu.make_async_copy(grad, grad_in, own_sem),
    ]
    for copy in copies:
        copy.start()
    for i, start in enumerate(range(done, width, chunk)):
        held[i, :, :] = lax.dot_general(
            x_all[:, pl.ds(start, chunk)], g_all[...], TN, preferred_element_type=jnp.float32)
        copies.append(pltpu.make_async_copy(held.at[i], weight_grad.at[pl.ds(start, chunk), :], sems.at[i]))
        copies[-1].start()
    for copy in copies:
        copy.wait()


def relay_kernel(
    weights, codes, scales, grad_out,
    grad_in, weight_part, x_all, g_all,
    w_buf, c_buf, r_buf, s_buf, x_buf, prod, from_left, from_right, from_end, stage,
    w_sem, c_sem, s_sem, g_sem, hop_send, hop_recv,
    sum_send, sum_recv, end_send, end_recv, stage_recv, carry_send,
    g_send, share_recv, g_recv, pass_send, pass_recv, x_send, x_recv,
    *, sections, shards, replicas,
):
    section, shard, replica = (lax.axis_index(n) for n in ("pipe", "tensor", "dp"))
    is_last = section == sections - 1
    tok, cols = grad_in.shape
    width = x_buf.shape[2]
    rows = tok // MICRO
    pairs = replicas // 2
    pair, side = replica // 2, lax.rem(replica, 2)
    sibling = 2 * pair + 1 - side
    at_left, at_right = shard == 0, shard == shards - 1
    at_end = at_left | at_right

    barrier = pltpu.get_barrier_semaphore()

    def greet(condition, target):
        @pl.when(condition)
        def _():
            pl.semaphore_signal(barrier, inc=1, device_id=target)

    def w_copy(j):
        part = pl.ds(pl.multiple_of(j * cols, cols), cols)
        return pltpu.make_async_copy(weights.at[part, :], w_buf.at[part, :], w_sem.at[j])

    def c_copy(o):
        peer = lax.rem(replica + o, replicas)
        part = pl.ds(pl.multiple_of(peer * width, width), width)
        return pltpu.make_async_copy(codes.at[:, part], c_buf.at[o], c_sem.at[o])

    def s_copy():
        return pltpu.make_async_copy(scales, r_buf, s_sem)

    def strip(m):
        return pl.ds(pl.multiple_of(m * rows, rows), rows)

    def held(source, m):
        return pl.ds(pl.multiple_of(source * tok + m * rows, rows), rows)

    def block(source):
        return pl.ds(pl.multiple_of(source * tok, tok), tok)

    def g_load():
        return pltpu.make_async_copy(grad_out, g_all.at[block(replica), :], g_sem)

    def order(i, far_first=False):
        step = jnp.where(at_end & (i < 2) & jnp.logical_not(far_first), 1 - i, i)
        return jnp.where(2 * shard < shards, shards - 1 - step, step)

    def load_codes():
        s_copy().start()

        @pl.loop(0, replicas)
        def _(i):
            c_copy(replicas - 1 - i).start()

    @pl.when(is_last)
    def _():
        g_load().start()

    @pl.when(jnp.logical_not(is_last))
    def _():
        load_codes()

    @pl.loop(0, shards)
    def _(i):
        w_copy(order(i)).start()

    greet(shard > 0, {"tensor": shard - 1})
    greet(shard < shards - 1, {"tensor": shard + 1})
    greet(at_end, {"tensor": shards - 1 - shard})
    greet(section > 0, {"pipe": section - 1})
    greet(section < sections - 1, {"pipe": section + 1})

    @pl.loop(1, replicas)
    def _(o):
        pl.semaphore_signal(barrier, inc=1, device_id={"dp": lax.rem(replica + o, replicas)})

    def one(condition):
        return jnp.where(condition, 1, 0)

    pl.semaphore_wait(
        barrier,
        replicas - 1 + one(shard > 0) + one(shard < shards - 1) + one(at_end) + one(section > 0)
        + one(section < sections - 1),
    )

    def hop(m):
        return pltpu.make_async_remote_copy(
            src_ref=grad_in.at[strip(m), :], dst_ref=g_all.at[held(replica, m), :],
            send_sem=hop_send, recv_sem=hop_recv.at[m], device_id={"pipe": section - 1})

    def to_right(m, j):
        return pltpu.make_async_remote_copy(
            src_ref=prod.at[j, strip(m), :], dst_ref=from_left.at[j, strip(m), :],
            send_sem=sum_send.at[j], recv_sem=sum_recv.at[m, j + 1], device_id={"tensor": shard + 1})

    def to_left(m, j):
        return pltpu.make_async_remote_copy(
            src_ref=prod.at[j, strip(m), :], dst_ref=from_right.at[j, strip(m), :],
            send_sem=sum_send.at[j], recv_sem=sum_recv.at[m, j], device_id={"tensor": shard - 1})

    def to_end(m):
        j = shards - 1 - shard
        return pltpu.make_async_remote_copy(
            src_ref=prod.at[j, strip(m), :], dst_ref=from_end.at[strip(m), :],
            send_sem=end_send, recv_sem=end_recv.at[m], device_id={"tensor": j})

    def detoured(m):
        return jnp.where(is_last, (m >= FILL) & (m < FULL), (m >= DRAIN) & (m < STOP))

    def to_stage(m, k):
        return pltpu.make_async_remote_copy(
            src_ref=prod.at[shards - 1 - shard, strip(m), :], dst_ref=stage.at[k, strip(m), :],
            send_sem=end_send, recv_sem=stage_recv.at[k, m - (FILL, DRAIN)[k]], device_id={"pipe": section + (2 * k - 1)})

    def carry(m, k):
        to_stage(m, k).wait_recv()
        pltpu.make_async_remote_copy(
            src_ref=stage.at[k, strip(m), :], dst_ref=from_end.at[strip(m), :],
            send_sem=carry_send.at[k], recv_sem=end_recv.at[m],
            device_id={"pipe": section + (1 - 2 * k), "tensor": shards - 1 - shard}).start()

    def carry_all(start, stop, k):
        @pl.loop(start, stop)
        def _(m):
            carry(m, k)

    def g_share(m):
        return pltpu.make_async_remote_copy(
            src_ref=g_all.at[held(replica, m), :], dst_ref=g_all.at[held(replica, m), :],
            send_sem=g_send.at[0], recv_sem=share_recv, device_id={"dp": sibling})

    def g_cross(m, o):
        return pltpu.make_async_remote_copy(
            src_ref=g_all.at[held(replica, m), :], dst_ref=g_all.at[held(replica, m), :],
            send_sem=g_send.at[o], recv_sem=g_recv.at[m, o - 1],
            device_id={"dp": 2 * lax.rem(pair + o, pairs) + side})

    def g_pass(m, o):
        source = 2 * lax.rem(pair + pairs - o, pairs) + side
        return pltpu.make_async_remote_copy(
            src_ref=g_all.at[held(source, m), :], dst_ref=g_all.at[held(source, m), :],
            send_sem=pass_send.at[o], recv_sem=pass_recv.at[o], device_id={"dp": sibling})

    def x_share(o):
        return pltpu.make_async_remote_copy(
            src_ref=x_buf.at[o], dst_ref=x_all.at[block(replica), :],
            send_sem=x_send.at[o], recv_sem=x_recv.at[o],
            device_id={"dp": lax.rem(replica + o, replicas)})

    def dequantize():
        s_copy().wait()
        s_buf[...] = jnp.transpose(jnp.broadcast_to(r_buf[...], (128, tok)))

        @pl.loop(0, replicas)
        def _(i):
            o = replicas - 1 - i
            c_copy(o).wait()

            @pl.loop(0, 4)
            def _(m):
                part = pl.ds(pl.multiple_of(m * (tok // 4), tok // 4), tok // 4)
                own = pl.ds(pl.multiple_of(replica * tok + m * (tok // 4), tok // 4), tok // 4)
                value = (c_buf[o, part, :].astype(jnp.float32) * s_buf[part, 0:1]).astype(jnp.bfloat16)

                @pl.when(o > 0)
                def _():
                    x_buf[o, part, :] = value

                @pl.when(o == 0)
                def _():
                    x_all[own, :] = value

            @pl.when(o > 0)
            def _():
                x_share(o).start()

    def launch(m, j):
        straight = j == shards - 1 - shard

        @pl.when(at_end & straight & jnp.logical_not(detoured(m)))
        def _():
            to_end(m).start()

        @pl.when(at_end & straight & detoured(m) & is_last)
        def _():
            to_stage(m, 0).start()

        @pl.when(at_end & straight & detoured(m) & jnp.logical_not(is_last))
        def _():
            to_stage(m, 1).start()

        @pl.when(at_left & (j > 0) & jnp.logical_not(straight))
        def _():
            to_right(m, j).start()

        @pl.when(at_right & (j < shards - 1) & jnp.logical_not(straight))
        def _():
            to_left(m, j).start()

    def launch_next(m):
        @pl.when(shard == 1)
        def _():
            to_right(m, shards - 1).start()

        @pl.when(shard == shards - 2)
        def _():
            to_left(m, 0).start()

    def spread(m):
        g_share(m).start()

        @pl.loop(1, pairs)
        def _(o):
            g_cross(m, o).start()

    def pass_on(m):
        @pl.loop(1, pairs)
        def _(o):
            g_cross(m, o).wait_recv()
            g_pass(m, o).start()

    def w_part(j):
        return w_buf[pl.ds(pl.multiple_of(j * cols, cols), cols), :]

    def produce_all():
        g_load().wait()

        @pl.loop(0, shards)
        def _(i):
            j = order(i)
            w_copy(j).wait()
            prod[j, :, :] = lax.dot_general(
                g_all[block(replica), :], w_part(j), NT, preferred_element_type=jnp.float32
            ).astype(jnp.bfloat16)
            launch(0, j)

            @pl.when(i == 0)
            def _():
                @pl.loop(0, LEAD)
                def _(m):
                    launch_next(m)

        @pl.when(at_end)
        def _():
            @pl.loop(1, MICRO)
            def _(m):
                @pl.loop(0, shards)
                def _(i):
                    launch(m, order(i))

    def produce(m):
        hop(m).wait_recv()
        spread(m)

        @pl.loop(0, shards)
        def _(i):
            j = order(i, detoured(m))
            prod[j, strip(m), :] = lax.dot_general(
                g_all[held(replica, m), :], w_part(j), NT, preferred_element_type=jnp.float32
            ).astype(jnp.bfloat16)
            launch(m, j)

            @pl.when(i == 0)
            def _():
                launch_next(m)

    def add_in(m, j, arrived):
        part = strip(m)
        total = prod[j, part, :].astype(jnp.float32) + arrived[j, part, :].astype(jnp.float32)
        prod[j, part, :] = total.astype(jnp.bfloat16)

    def relay(m, rightward):
        @pl.loop(0, shards - 1)
        def _(i):
            far = shards - 1 - i
            right, left = shard + far, shard - far

            @pl.when(rightward & (shard > 0) & (right < shards) & ((shard > 1) | (right < shards - 1)))
            def _():
                to_right(m, right).wait_recv()
                add_in(m, right, from_left)
                to_right(m, right).start()

            @pl.when(jnp.logical_not(rightward) & (shard < shards - 1) & (left >= 0) & ((shard < shards - 2) | (left > 0)))
            def _():
                to_left(m, left).wait_recv()
                add_in(m, left, from_right)
                to_left(m, left).start()

    def finish(m):
        part = strip(m)

        @pl.when(shard > 0)
        def _():
            to_right(m, shard).wait_recv()

        @pl.when(shard < shards - 1)
        def _():
            to_left(m, shard).wait_recv()

        @pl.when(at_end)
        def _():
            to_end(m).wait_recv()

        def of(ref):
            return ref[shard, part, :].astype(jnp.float32)

        own = of(prod) + g_all[held(replica, m), :].astype(jnp.float32)

        @pl.when(jnp.logical_not(at_end))
        def _():
            grad_in[part, :] = (own + (of(from_left) + of(from_right))).astype(jnp.bfloat16)

        def settle(condition, inner):
            @pl.when(condition)
            def _():
                grad_in[part, :] = (own + (of(inner) + from_end[part, :].astype(jnp.float32))).astype(jnp.bfloat16)

        settle(at_left, from_right)
        settle(at_right, from_left)

        @pl.when(section > 0)
        def _():
            hop(m).start()

    near = 2 * shard < shards
    late = jnp.where(at_end, END_LATE, MID_LATE)

    def relays(m):
        relay(m, near)
        relay(m, jnp.logical_not(near))

    @pl.when(is_last)
    def _():
        produce_all()

        @pl.loop(0, MICRO)
        def _(m):
            @pl.when(jnp.logical_not(at_end))
            def _():
                relays(m)

                @pl.when(m + LEAD < MICRO)
                def _():
                    launch_next(m + LEAD)

            @pl.when(m == 0)
            def _():
                load_codes()

                @pl.loop(0, MICRO)
                def _(n):
                    spread(n)

            @pl.when(at_end)
            def _():
                finish(m)

            @pl.when(jnp.logical_not(at_end))
            def _():
                @pl.when(m < PROMPT)
                def _():
                    finish(m)

                @pl.when(m >= PROMPT + WAIT)
                def _():
                    finish(m - WAIT)

            @pl.when(m == CODES_AT)
            def _():
                dequantize()

        @pl.when(jnp.logical_not(at_end))
        def _():
            @pl.loop(MICRO - WAIT, MICRO)
            def _(m):
                finish(m)

        @pl.loop(0, MICRO)
        def _(m):
            pass_on(m)

    below, above = at_end & (section > 0), at_end & (section == sections - 2)

    @pl.when(jnp.logical_not(is_last))
    def _():
        dequantize()

        @pl.when(above)
        def _():
            carry_all(FILL, FULL, 0)

        @pl.loop(0, shards)
        def _(i):
            w_copy(order(i)).wait()

        behind = jnp.where(at_end, END_LAG, MID_LAG)

        @pl.loop(0, MICRO)
        def _(s):
            def at(lag, action):
                @pl.when(s >= lag)
                def _():
                    action(s - lag)

            produce(s)
            at(NEAR_LAG, lambda m: relay(m, near))
            at(FAR_LAG, lambda m: relay(m, jnp.logical_not(near)))
            at(PASS_LAG, pass_on)
            at(behind, finish)

        @pl.loop(MICRO - NEAR_LAG, MICRO)
        def _(m):
            relay(m, near)

        @pl.loop(MICRO - FAR_LAG, MICRO)
        def _(m):
            relay(m, jnp.logical_not(near))

        @pl.loop(MICRO - PASS_LAG, MICRO)
        def _(m):
            pass_on(m)

        @pl.loop(MICRO - behind, MICRO - late)
        def _(m):
            finish(m)

    @pl.when(below)
    def _():
        carry_all(DRAIN, STOP, 1)

    @pl.loop(1, replicas)
    def _(o):
        x_share(o).wait_recv()

    def sent(source, sem):
        pltpu.make_async_copy(source, source, sem).wait()

    sent(g_all.at[block(sibling), :], share_recv)

    @pl.loop(1, pairs)
    def _(o):
        sent(g_all.at[block(2 * lax.rem(pair + pairs - o, pairs) + 1 - side), :], pass_recv.at[o])

    chunk = rows_a_step(width)

    @pl.loop(0, weight_part.shape[0] // chunk)
    def _(i):
        part = pl.ds(pl.multiple_of(i * chunk, chunk), chunk)
        weight_part[part, :] = lax.dot_general(x_all[:, part], g_all[...], TN, preferred_element_type=jnp.float32)

    @pl.when(jnp.logical_not(is_last))
    def _():
        @pl.loop(MICRO - late, MICRO)
        def _(m):
            finish(m)

    @pl.loop(0, shards)
    def _(j):
        @pl.when((j != shard) & jnp.logical_not(at_end & (j == shards - 1 - shard)))
        def _():
            sent(prod.at[j], sum_send.at[j])

    @pl.when(at_end)
    def _():
        sent(prod.at[shards - 1 - shard], end_send)

    @pl.when(above)
    def _():
        sent(stage.at[0, pl.ds(0, (FULL - FILL) * rows), :], carry_send.at[0])

    @pl.when(below)
    def _():
        sent(stage.at[1, pl.ds(0, (STOP - DRAIN) * rows), :], carry_send.at[1])

    @pl.when(section > 0)
    def _():
        sent(grad_in, hop_send)

    sent(g_all.at[block(replica), :], g_send.at[0])

    @pl.loop(1, pairs)
    def _(o):
        sent(g_all.at[block(replica), :], g_send.at[o])
        sent(g_all.at[block(replica), :], pass_send.at[o])

    @pl.loop(1, replicas)
    def _(o):
        x_share(o).wait_send()


def per_device(weights, codes, scales, grad_out):
    sections, shards, replicas = (lax.axis_size(n) for n in ("pipe", "tensor", "dp"))
    tok, cols = grad_out.shape
    depth = weights.shape[1]
    width = depth // replicas
    pairs = replicas // 2
    low = jnp.bfloat16
    dma = pltpu.SemaphoreType.DMA
    far = pl.BlockSpec(memory_space=pltpu.MemorySpace.HBM)
    inside = pl.BlockSpec(memory_space=pltpu.VMEM)
    chunk = rows_a_step(width)
    done = min(KEPT, width // chunk - 1) * chunk
    later = (width - done) // chunk
    handed = pl.pallas_call(
        functools.partial(relay_kernel, sections=sections, shards=shards, replicas=replicas),
        out_shape=(
            pltpu.VMEM((tok, cols), low),
            pltpu.VMEM((done, cols), jnp.float32),
            pltpu.VMEM((replicas * tok, width), low),
            pltpu.VMEM((replicas * tok, cols), low),
        ),
        in_specs=[far, far, far, far],
        out_specs=(inside,) * 4,
        scratch_shapes=[
            pltpu.VMEM((depth, cols), low),
            pltpu.VMEM((replicas, tok, width), jnp.int32),
            pltpu.VMEM((1, tok), jnp.float32),
            pltpu.VMEM((tok, 128), jnp.float32),
            pltpu.VMEM((replicas, tok, width), low),
            pltpu.VMEM((shards, tok, cols), low),
            pltpu.VMEM((shards, tok, cols), low),
            pltpu.VMEM((shards, tok, cols), low),
            pltpu.VMEM((tok, cols), low),
            pltpu.VMEM((2, tok, cols), low),
            dma((shards,)), dma((replicas,)), dma(()), dma(()), dma(()), dma((MICRO,)),
            dma((shards,)), dma((MICRO, shards + 1)), dma(()), dma((MICRO,)), dma((2, max(FULL - FILL, STOP - DRAIN))), dma((2,)),
            dma((pairs,)), dma(()), dma((MICRO, pairs - 1)), dma((pairs,)), dma((pairs,)),
            dma((replicas,)), dma((replicas,)),
        ],
        compiler_params=pltpu.CompilerParams(collective_id=0, has_side_effects=True, vmem_limit_bytes=57 * 2**20),
    )(weights[0], codes[0], scales, grad_out)
    grad_in, weight_grad = pl.pallas_call(
        closing_kernel,
        out_shape=(
            jax.ShapeDtypeStruct((tok, cols), low),
            jax.ShapeDtypeStruct((width, cols), jnp.float32),
        ),
        in_specs=[inside] * 4,
        out_specs=(far, far),
        scratch_shapes=[pltpu.VMEM((later, chunk, cols), jnp.float32), dma((later,)), dma(()), dma(())],
        compiler_params=pltpu.CompilerParams(vmem_limit_bytes=LIMIT * 2**20),
    )(*handed)
    return grad_in[None], weight_grad[None]


def solution(mesh):
    placed = (P("pipe", None, "tensor"), P("pipe", "dp", None), P("pipe", "dp"), P("dp", "tensor"))
    return jax.shard_map(
        per_device,
        mesh=mesh,
        in_specs=placed,
        out_specs=(P("pipe", "dp", "tensor"), P("pipe", "dp", "tensor")),
        check_vma=False,
    )
```

```python
import functools

import jax
import jax.numpy as jnp
from jax import lax
from jax.experimental import pallas as pl
from jax.experimental.pallas import tpu as pltpu
from jax.sharding import PartitionSpec as P

MICRO = 8
NEAR_LAG, FAR_LAG, MID_LAG, END_LAG, PASS_LAG = 1, 1, 3, 4, 4
MID_LATE, END_LATE = 3, 4
CODES_AT = 1
PROMPT, WAIT = 1, 1
FILL, FULL = 1, 5
DRAIN, STOP = 4, 8
LEAD = 2
STEPS, KEPT = 4, 2
LIMIT = 32
FAR_AT = 2
NT = (((1,), (1,)), ((), ()))
TN = (((0,), (0,)), ((), ()))


def rows_a_step(width):
    return max(width // STEPS, 128)


def closing_kernel(grad, part, x_all, g_all, grad_in, weight_grad, held, sems, own_sem, part_sem):
    done, width = part.shape[0], x_all.shape[1]
    chunk = rows_a_step(width)
    copies = [
        pltpu.make_async_copy(part, weight_grad.at[pl.ds(0, done), :], part_sem),
        pltpu.make_async_copy(grad, grad_in, own_sem),
    ]
    for copy in copies:
        copy.start()
    for i, start in enumerate(range(done, width, chunk)):
        held[i, :, :] = lax.dot_general(
            x_all[:, pl.ds(start, chunk)], g_all[...], TN, preferred_element_type=jnp.float32)
        copies.append(pltpu.make_async_copy(held.at[i], weight_grad.at[pl.ds(start, chunk), :], sems.at[i]))
        copies[-1].start()
    for copy in copies:
        copy.wait()


def relay_kernel(
    weights, codes, scales, grad_out,
    grad_in, weight_part, x_all, g_all,
    w_buf, c_buf, r_buf, s_buf, x_buf, prod, from_left, from_right, from_end, stage,
    w_sem, c_sem, s_sem, g_sem, hop_send, hop_recv,
    sum_send, sum_recv, end_send, end_recv, stage_recv, carry_send,
    g_send, share_recv, g_recv, pass_send, pass_recv, x_send, x_recv,
    *, sections, shards, replicas,
):
    section, shard, replica = (lax.axis_index(n) for n in ("pipe", "tensor", "dp"))
    is_last = section == sections - 1
    tok, cols = grad_in.shape
    width = x_buf.shape[2]
    rows = tok // MICRO
    pairs = replicas // 2
    pair, side = replica // 2, lax.rem(replica, 2)
    sibling = 2 * pair + 1 - side
    at_left, at_right = shard == 0, shard == shards - 1
    at_end = at_left | at_right
    near = 2 * shard < shards
    one_step = shards <= 4

    barrier = pltpu.get_barrier_semaphore()

    def greet(condition, target):
        @pl.when(condition)
        def _():
            pl.semaphore_signal(barrier, inc=1, device_id=target)

    def w_copy(j):
        part = pl.ds(pl.multiple_of(j * cols, cols), cols)
        return pltpu.make_async_copy(weights.at[part, :], w_buf.at[part, :], w_sem.at[j])

    def c_copy(o):
        peer = lax.rem(replica + o, replicas)
        part = pl.ds(pl.multiple_of(peer * width, width), width)
        return pltpu.make_async_copy(codes.at[:, part], c_buf.at[o], c_sem.at[o])

    def s_copy():
        return pltpu.make_async_copy(scales, r_buf, s_sem)

    def strip(m):
        return pl.ds(pl.multiple_of(m * rows, rows), rows)

    def held(source, m):
        return pl.ds(pl.multiple_of(source * tok + m * rows, rows), rows)

    def block(source):
        return pl.ds(pl.multiple_of(source * tok, tok), tok)

    def g_load():
        return pltpu.make_async_copy(grad_out, g_all.at[block(replica), :], g_sem)

    def order(i, far_first=False):
        step = jnp.where(at_end & (i < 2) & jnp.logical_not(far_first), 1 - i, i)
        return jnp.where(2 * shard < shards, shards - 1 - step, step)

    def load_codes():
        s_copy().start()

        @pl.loop(0, replicas)
        def _(i):
            c_copy(replicas - 1 - i).start()

    @pl.when(is_last)
    def _():
        g_load().start()

    @pl.when(jnp.logical_not(is_last))
    def _():
        load_codes()

    @pl.loop(0, shards)
    def _(i):
        w_copy(order(i)).start()

    greet(shard > 0, {"tensor": shard - 1})
    greet(shard < shards - 1, {"tensor": shard + 1})
    greet(at_end, {"tensor": shards - 1 - shard})
    greet(section > 0, {"pipe": section - 1})
    greet(section < sections - 1, {"pipe": section + 1})

    @pl.loop(1, replicas)
    def _(o):
        pl.semaphore_signal(barrier, inc=1, device_id={"dp": lax.rem(replica + o, replicas)})

    def one(condition):
        return jnp.where(condition, 1, 0)

    pl.semaphore_wait(
        barrier,
        replicas - 1 + one(shard > 0) + one(shard < shards - 1) + one(at_end) + one(section > 0)
        + one(section < sections - 1),
    )

    def hop(m):
        return pltpu.make_async_remote_copy(
            src_ref=grad_in.at[strip(m), :], dst_ref=g_all.at[held(replica, m), :],
            send_sem=hop_send, recv_sem=hop_recv.at[m], device_id={"pipe": section - 1})

    def to_right(m, j):
        return pltpu.make_async_remote_copy(
            src_ref=prod.at[j, strip(m), :], dst_ref=from_left.at[j, strip(m), :],
            send_sem=sum_send.at[j], recv_sem=sum_recv.at[m, j + 1], device_id={"tensor": shard + 1})

    def to_left(m, j):
        return pltpu.make_async_remote_copy(
            src_ref=prod.at[j, strip(m), :], dst_ref=from_right.at[j, strip(m), :],
            send_sem=sum_send.at[j], recv_sem=sum_recv.at[m, j], device_id={"tensor": shard - 1})

    def to_end(m):
        j = shards - 1 - shard
        return pltpu.make_async_remote_copy(
            src_ref=prod.at[j, strip(m), :], dst_ref=from_end.at[strip(m), :],
            send_sem=end_send, recv_sem=end_recv.at[m], device_id={"tensor": j})

    def detoured(m):
        return jnp.where(is_last, (m >= FILL) & (m < FULL), (m >= DRAIN) & (m < STOP))

    def to_stage(m, k):
        return pltpu.make_async_remote_copy(
            src_ref=prod.at[shards - 1 - shard, strip(m), :], dst_ref=stage.at[k, strip(m), :],
            send_sem=end_send, recv_sem=stage_recv.at[k, m - (FILL, DRAIN)[k]], device_id={"pipe": section + (2 * k - 1)})

    def carry(m, k):
        to_stage(m, k).wait_recv()
        pltpu.make_async_remote_copy(
            src_ref=stage.at[k, strip(m), :], dst_ref=from_end.at[strip(m), :],
            send_sem=carry_send.at[k], recv_sem=end_recv.at[m],
            device_id={"pipe": section + (1 - 2 * k), "tensor": shards - 1 - shard}).start()

    def carry_all(start, stop, k):
        @pl.loop(start, stop)
        def _(m):
            carry(m, k)

    def g_share(m):
        return pltpu.make_async_remote_copy(
            src_ref=g_all.at[held(replica, m), :], dst_ref=g_all.at[held(replica, m), :],
            send_sem=g_send.at[0], recv_sem=share_recv, device_id={"dp": sibling})

    def g_cross(m, o):
        return pltpu.make_async_remote_copy(
            src_ref=g_all.at[held(replica, m), :], dst_ref=g_all.at[held(replica, m), :],
            send_sem=g_send.at[o], recv_sem=g_recv.at[m, o - 1],
            device_id={"dp": 2 * lax.rem(pair + o, pairs) + side})

    def g_pass(m, o):
        source = 2 * lax.rem(pair + pairs - o, pairs) + side
        return pltpu.make_async_remote_copy(
            src_ref=g_all.at[held(source, m), :], dst_ref=g_all.at[held(source, m), :],
            send_sem=pass_send.at[o], recv_sem=pass_recv.at[o], device_id={"dp": sibling})

    def x_share(o):
        return pltpu.make_async_remote_copy(
            src_ref=x_buf.at[o], dst_ref=x_all.at[block(replica), :],
            send_sem=x_send.at[o], recv_sem=x_recv.at[o],
            device_id={"dp": lax.rem(replica + o, replicas)})

    def dequantize():
        s_copy().wait()
        s_buf[...] = jnp.transpose(jnp.broadcast_to(r_buf[...], (128, tok)))

        @pl.loop(0, replicas)
        def _(i):
            o = replicas - 1 - i
            c_copy(o).wait()

            @pl.loop(0, 4)
            def _(m):
                part = pl.ds(pl.multiple_of(m * (tok // 4), tok // 4), tok // 4)
                own = pl.ds(pl.multiple_of(replica * tok + m * (tok // 4), tok // 4), tok // 4)
                value = (c_buf[o, part, :].astype(jnp.float32) * s_buf[part, 0:1]).astype(jnp.bfloat16)

                @pl.when(o > 0)
                def _():
                    x_buf[o, part, :] = value

                @pl.when(o == 0)
                def _():
                    x_all[own, :] = value

            @pl.when(o > 0)
            def _():
                x_share(o).start()

    def launch(m, j):
        straight = j == shards - 1 - shard

        @pl.when(at_end & straight & jnp.logical_not(detoured(m)))
        def _():
            to_end(m).start()

        @pl.when(at_end & straight & detoured(m) & is_last)
        def _():
            to_stage(m, 0).start()

        @pl.when(at_end & straight & detoured(m) & jnp.logical_not(is_last))
        def _():
            to_stage(m, 1).start()

        @pl.when(at_left & (j > 0) & jnp.logical_not(straight))
        def _():
            to_right(m, j).start()

        @pl.when(at_right & (j < shards - 1) & jnp.logical_not(straight))
        def _():
            to_left(m, j).start()

    def launch_next(m):
        @pl.when(shard == 1)
        def _():
            to_right(m, shards - 1).start()

        @pl.when(shard == shards - 2)
        def _():
            to_left(m, 0).start()

    def spread(m):
        g_share(m).start()

        @pl.loop(1, pairs)
        def _(o):
            g_cross(m, o).start()

    def pass_on(m):
        @pl.loop(1, pairs)
        def _(o):
            g_cross(m, o).wait_recv()
            g_pass(m, o).start()

    def w_part(j):
        return w_buf[pl.ds(pl.multiple_of(j * cols, cols), cols), :]

    def produce_all():
        g_load().wait()

        @pl.loop(0, shards)
        def _(i):
            j = order(i)
            w_copy(j).wait()
            prod[j, :, :] = lax.dot_general(
                g_all[block(replica), :], w_part(j), NT, preferred_element_type=jnp.float32
            ).astype(jnp.bfloat16)
            launch(0, j)

            @pl.when(i == 0)
            def _():
                @pl.loop(0, LEAD)
                def _(m):
                    launch_next(m)

        @pl.when(at_end)
        def _():
            @pl.loop(1, MICRO)
            def _(m):
                @pl.loop(0, shards)
                def _(i):
                    launch(m, order(i))

    def produce(m):
        hop(m).wait_recv()
        spread(m)

        @pl.loop(0, shards)
        def _(i):
            j = order(i, detoured(m))
            prod[j, strip(m), :] = lax.dot_general(
                g_all[held(replica, m), :], w_part(j), NT, preferred_element_type=jnp.float32
            ).astype(jnp.bfloat16)
            launch(m, j)

            @pl.when(i == 0)
            def _():
                launch_next(m)

            if one_step:
                @pl.when((i == FAR_AT) & (m >= FAR_LAG))
                def _():
                    relay(m - FAR_LAG, jnp.logical_not(near))

    def add_in(m, j, arrived):
        part = strip(m)
        total = prod[j, part, :].astype(jnp.float32) + arrived[j, part, :].astype(jnp.float32)
        prod[j, part, :] = total.astype(jnp.bfloat16)

    def relay(m, rightward):
        @pl.loop(0, shards - 1)
        def _(i):
            far = shards - 1 - i
            right, left = shard + far, shard - far

            @pl.when(rightward & (shard > 0) & (right < shards) & ((shard > 1) | (right < shards - 1)))
            def _():
                to_right(m, right).wait_recv()
                add_in(m, right, from_left)
                to_right(m, right).start()

            @pl.when(jnp.logical_not(rightward) & (shard < shards - 1) & (left >= 0) & ((shard < shards - 2) | (left > 0)))
            def _():
                to_left(m, left).wait_recv()
                add_in(m, left, from_right)
                to_left(m, left).start()

    def finish(m):
        part = strip(m)

        @pl.when(shard > 0)
        def _():
            to_right(m, shard).wait_recv()

        @pl.when(shard < shards - 1)
        def _():
            to_left(m, shard).wait_recv()

        @pl.when(at_end)
        def _():
            to_end(m).wait_recv()

        def of(ref):
            return ref[shard, part, :].astype(jnp.float32)

        own = of(prod) + g_all[held(replica, m), :].astype(jnp.float32)

        @pl.when(jnp.logical_not(at_end))
        def _():
            grad_in[part, :] = (own + (of(from_left) + of(from_right))).astype(jnp.bfloat16)

        def settle(condition, inner):
            @pl.when(condition)
            def _():
                grad_in[part, :] = (own + (of(inner) + from_end[part, :].astype(jnp.float32))).astype(jnp.bfloat16)

        settle(at_left, from_right)
        settle(at_right, from_left)

        @pl.when(section > 0)
        def _():
            hop(m).start()

    late = jnp.where(at_end, END_LATE, MID_LATE)

    def relays(m):
        relay(m, near)
        relay(m, jnp.logical_not(near))

    @pl.when(is_last)
    def _():
        produce_all()

        @pl.loop(0, MICRO)
        def _(m):
            @pl.when(jnp.logical_not(at_end))
            def _():
                relays(m)

                @pl.when(m + LEAD < MICRO)
                def _():
                    launch_next(m + LEAD)

            @pl.when(m == 0)
            def _():
                load_codes()

                @pl.loop(0, MICRO)
                def _(n):
                    spread(n)

            @pl.when(at_end)
            def _():
                finish(m)

            @pl.when(jnp.logical_not(at_end))
            def _():
                @pl.when(m < PROMPT)
                def _():
                    finish(m)

                @pl.when(m >= PROMPT + WAIT)
                def _():
                    finish(m - WAIT)

            @pl.when(m == CODES_AT)
            def _():
                dequantize()

        @pl.when(jnp.logical_not(at_end))
        def _():
            @pl.loop(MICRO - WAIT, MICRO)
            def _(m):
                finish(m)

        @pl.loop(0, MICRO)
        def _(m):
            pass_on(m)

    below, above = at_end & (section > 0), at_end & (section == sections - 2)

    @pl.when(jnp.logical_not(is_last))
    def _():
        dequantize()

        @pl.when(above)
        def _():
            carry_all(FILL, FULL, 0)

        @pl.loop(0, shards)
        def _(i):
            w_copy(order(i)).wait()

        behind = jnp.where(at_end, END_LAG, MID_LAG)

        @pl.loop(0, MICRO)
        def _(s):
            def at(lag, action):
                @pl.when(s >= lag)
                def _():
                    action(s - lag)

            produce(s)
            at(NEAR_LAG, lambda m: relay(m, near))
            if not one_step:
                at(FAR_LAG, lambda m: relay(m, jnp.logical_not(near)))
            at(PASS_LAG, pass_on)
            at(behind, finish)

        for rightward in (jnp.logical_not(near), near) if one_step else (near, jnp.logical_not(near)):
            @pl.loop(MICRO - 1, MICRO)
            def _(m):
                relay(m, rightward)

        @pl.loop(MICRO - PASS_LAG, MICRO)
        def _(m):
            pass_on(m)

        @pl.loop(MICRO - behind, MICRO - late)
        def _(m):
            finish(m)

    @pl.when(below)
    def _():
        carry_all(DRAIN, STOP, 1)

    @pl.loop(1, replicas)
    def _(o):
        x_share(o).wait_recv()

    def sent(source, sem):
        pltpu.make_async_copy(source, source, sem).wait()

    sent(g_all.at[block(sibling), :], share_recv)

    @pl.loop(1, pairs)
    def _(o):
        sent(g_all.at[block(2 * lax.rem(pair + pairs - o, pairs) + 1 - side), :], pass_recv.at[o])

    chunk = rows_a_step(width)

    @pl.loop(0, weight_part.shape[0] // chunk)
    def _(i):
        part = pl.ds(pl.multiple_of(i * chunk, chunk), chunk)
        weight_part[part, :] = lax.dot_general(x_all[:, part], g_all[...], TN, preferred_element_type=jnp.float32)

    @pl.when(jnp.logical_not(is_last))
    def _():
        @pl.loop(MICRO - late, MICRO)
        def _(m):
            finish(m)

    @pl.loop(0, shards)
    def _(j):
        @pl.when((j != shard) & jnp.logical_not(at_end & (j == shards - 1 - shard)))
        def _():
            sent(prod.at[j], sum_send.at[j])

    @pl.when(at_end)
    def _():
        sent(prod.at[shards - 1 - shard], end_send)

    @pl.when(above)
    def _():
        sent(stage.at[0, pl.ds(0, (FULL - FILL) * rows), :], carry_send.at[0])

    @pl.when(below)
    def _():
        sent(stage.at[1, pl.ds(0, (STOP - DRAIN) * rows), :], carry_send.at[1])

    @pl.when(section > 0)
    def _():
        sent(grad_in, hop_send)

    sent(g_all.at[block(replica), :], g_send.at[0])

    @pl.loop(1, pairs)
    def _(o):
        sent(g_all.at[block(replica), :], g_send.at[o])
        sent(g_all.at[block(replica), :], pass_send.at[o])

    @pl.loop(1, replicas)
    def _(o):
        x_share(o).wait_send()


def per_device(weights, codes, scales, grad_out):
    sections, shards, replicas = (lax.axis_size(n) for n in ("pipe", "tensor", "dp"))
    tok, cols = grad_out.shape
    depth = weights.shape[1]
    width = depth // replicas
    pairs = replicas // 2
    low = jnp.bfloat16
    dma = pltpu.SemaphoreType.DMA
    far = pl.BlockSpec(memory_space=pltpu.MemorySpace.HBM)
    inside = pl.BlockSpec(memory_space=pltpu.VMEM)
    chunk = rows_a_step(width)
    done = min(KEPT, width // chunk - 1) * chunk
    later = (width - done) // chunk
    handed = pl.pallas_call(
        functools.partial(relay_kernel, sections=sections, shards=shards, replicas=replicas),
        out_shape=(
            pltpu.VMEM((tok, cols), low),
            pltpu.VMEM((done, cols), jnp.float32),
            pltpu.VMEM((replicas * tok, width), low),
            pltpu.VMEM((replicas * tok, cols), low),
        ),
        in_specs=[far, far, far, far],
        out_specs=(inside,) * 4,
        scratch_shapes=[
            pltpu.VMEM((depth, cols), low),
            pltpu.VMEM((replicas, tok, width), jnp.int32),
            pltpu.VMEM((1, tok), jnp.float32),
            pltpu.VMEM((tok, 128), jnp.float32),
            pltpu.VMEM((replicas, tok, width), low),
            pltpu.VMEM((shards, tok, cols), low),
            pltpu.VMEM((shards, tok, cols), low),
            pltpu.VMEM((shards, tok, cols), low),
            pltpu.VMEM((tok, cols), low),
            pltpu.VMEM((2, tok, cols), low),
            dma((shards,)), dma((replicas,)), dma(()), dma(()), dma(()), dma((MICRO,)),
            dma((shards,)), dma((MICRO, shards + 1)), dma(()), dma((MICRO,)), dma((2, max(FULL - FILL, STOP - DRAIN))), dma((2,)),
            dma((pairs,)), dma(()), dma((MICRO, pairs - 1)), dma((pairs,)), dma((pairs,)),
            dma((replicas,)), dma((replicas,)),
        ],
        compiler_params=pltpu.CompilerParams(collective_id=0, has_side_effects=True, vmem_limit_bytes=57 * 2**20),
    )(weights[0], codes[0], scales, grad_out)
    grad_in, weight_grad = pl.pallas_call(
        closing_kernel,
        out_shape=(
            jax.ShapeDtypeStruct((tok, cols), low),
            jax.ShapeDtypeStruct((width, cols), jnp.float32),
        ),
        in_specs=[inside] * 4,
        out_specs=(far, far),
        scratch_shapes=[pltpu.VMEM((later, chunk, cols), jnp.float32), dma((later,)), dma(()), dma(())],
        compiler_params=pltpu.CompilerParams(vmem_limit_bytes=LIMIT * 2**20),
    )(*handed)
    return grad_in[None], weight_grad[None]


def solution(mesh):
    placed = (P("pipe", None, "tensor"), P("pipe", "dp", None), P("pipe", "dp"), P("dp", "tensor"))
    return jax.shard_map(
        per_device,
        mesh=mesh,
        in_specs=placed,
        out_specs=(P("pipe", "dp", "tensor"), P("pipe", "dp", "tensor")),
        check_vma=False,
    )
```

```python
import functools

import jax
import jax.numpy as jnp
from jax import lax
from jax.experimental import pallas as pl
from jax.experimental.pallas import tpu as pltpu
from jax.sharding import PartitionSpec as P

MICRO = 8
NEAR_LAG, FAR_LAG, MID_LAG, END_LAG, PASS_LAG = 1, 1, 3, 4, 4
MID_LATE, END_LATE = 3, 4
CODES_AT = 1
PROMPT, WAIT = 1, 1
FILL, FULL = 1, 5
DRAIN, STOP = 4, 8
LEAD = 2
STEPS, KEPT = 8, 5
LIMIT = 32
NT = (((1,), (1,)), ((), ()))
TN = (((0,), (0,)), ((), ()))


def rows_a_step(width):
    return max(width // STEPS, 128)


def closing_kernel(grad, part, x_all, g_all, grad_in, weight_grad, held, sems, own_sem, part_sem):
    done, width = part.shape[0], x_all.shape[1]
    chunk = rows_a_step(width)
    copies = [
        pltpu.make_async_copy(part, weight_grad.at[pl.ds(0, done), :], part_sem),
        pltpu.make_async_copy(grad, grad_in, own_sem),
    ]
    for copy in copies:
        copy.start()
    for i, start in enumerate(range(done, width, chunk)):
        held[i, :, :] = lax.dot_general(
            x_all[:, pl.ds(start, chunk)], g_all[...], TN, preferred_element_type=jnp.float32)
        copies.append(pltpu.make_async_copy(held.at[i], weight_grad.at[pl.ds(start, chunk), :], sems.at[i]))
        copies[-1].start()
    for copy in copies:
        copy.wait()


def relay_kernel(
    weights, codes, scales, grad_out,
    grad_in, weight_part, x_all, g_all,
    w_buf, c_buf, r_buf, s_buf, x_buf, prod, from_left, from_right, from_end, stage,
    w_sem, c_sem, s_sem, g_sem, hop_send, hop_recv,
    sum_send, sum_recv, end_send, end_recv, stage_recv, carry_send,
    g_send, share_recv, g_recv, pass_send, pass_recv, x_send, x_recv,
    *, sections, shards, replicas,
):
    section, shard, replica = (lax.axis_index(n) for n in ("pipe", "tensor", "dp"))
    is_last = section == sections - 1
    tok, cols = grad_in.shape
    width = x_buf.shape[2]
    rows = tok // MICRO
    pairs = replicas // 2
    pair, side = replica // 2, lax.rem(replica, 2)
    sibling = 2 * pair + 1 - side
    at_left, at_right = shard == 0, shard == shards - 1
    at_end = at_left | at_right

    barrier = pltpu.get_barrier_semaphore()

    def greet(condition, target):
        @pl.when(condition)
        def _():
            pl.semaphore_signal(barrier, inc=1, device_id=target)

    def w_copy(j):
        part = pl.ds(pl.multiple_of(j * cols, cols), cols)
        return pltpu.make_async_copy(weights.at[part, :], w_buf.at[part, :], w_sem.at[j])

    def c_copy(o):
        peer = lax.rem(replica + o, replicas)
        part = pl.ds(pl.multiple_of(peer * width, width), width)
        return pltpu.make_async_copy(codes.at[:, part], c_buf.at[o], c_sem.at[o])

    def s_copy():
        return pltpu.make_async_copy(scales, r_buf, s_sem)

    def strip(m):
        return pl.ds(pl.multiple_of(m * rows, rows), rows)

    def held(source, m):
        return pl.ds(pl.multiple_of(source * tok + m * rows, rows), rows)

    def block(source):
        return pl.ds(pl.multiple_of(source * tok, tok), tok)

    def g_load():
        return pltpu.make_async_copy(grad_out, g_all.at[block(replica), :], g_sem)

    def order(i):
        step = jnp.where(at_end & (i < 2), 1 - i, i)
        return jnp.where(2 * shard < shards, shards - 1 - step, step)

    def load_codes():
        s_copy().start()

        @pl.loop(0, replicas)
        def _(i):
            c_copy(replicas - 1 - i).start()

    @pl.when(is_last)
    def _():
        g_load().start()

    @pl.when(jnp.logical_not(is_last))
    def _():
        load_codes()

    @pl.loop(0, shards)
    def _(i):
        w_copy(order(i)).start()

    greet(shard > 0, {"tensor": shard - 1})
    greet(shard < shards - 1, {"tensor": shard + 1})
    greet(at_end, {"tensor": shards - 1 - shard})
    greet(section > 0, {"pipe": section - 1})
    greet(section < sections - 1, {"pipe": section + 1})

    @pl.loop(1, replicas)
    def _(o):
        pl.semaphore_signal(barrier, inc=1, device_id={"dp": lax.rem(replica + o, replicas)})

    def one(condition):
        return jnp.where(condition, 1, 0)

    pl.semaphore_wait(
        barrier,
        replicas - 1 + one(shard > 0) + one(shard < shards - 1) + one(at_end) + one(section > 0)
        + one(section < sections - 1),
    )

    def hop(m):
        return pltpu.make_async_remote_copy(
            src_ref=grad_in.at[strip(m), :], dst_ref=g_all.at[held(replica, m), :],
            send_sem=hop_send, recv_sem=hop_recv.at[m], device_id={"pipe": section - 1})

    def to_right(m, j):
        return pltpu.make_async_remote_copy(
            src_ref=prod.at[j, strip(m), :], dst_ref=from_left.at[j, strip(m), :],
            send_sem=sum_send.at[j], recv_sem=sum_recv.at[m, j + 1], device_id={"tensor": shard + 1})

    def to_left(m, j):
        return pltpu.make_async_remote_copy(
            src_ref=prod.at[j, strip(m), :], dst_ref=from_right.at[j, strip(m), :],
            send_sem=sum_send.at[j], recv_sem=sum_recv.at[m, j], device_id={"tensor": shard - 1})

    def to_end(m):
        j = shards - 1 - shard
        return pltpu.make_async_remote_copy(
            src_ref=prod.at[j, strip(m), :], dst_ref=from_end.at[strip(m), :],
            send_sem=end_send, recv_sem=end_recv.at[m], device_id={"tensor": j})

    def detoured(m):
        return jnp.where(is_last, (m >= FILL) & (m < FULL), (m >= DRAIN) & (m < STOP))

    def to_stage(m, k):
        return pltpu.make_async_remote_copy(
            src_ref=prod.at[shards - 1 - shard, strip(m), :], dst_ref=stage.at[k, strip(m), :],
            send_sem=end_send, recv_sem=stage_recv.at[k, m - (FILL, DRAIN)[k]], device_id={"pipe": section + (2 * k - 1)})

    def carry(m, k):
        to_stage(m, k).wait_recv()
        pltpu.make_async_remote_copy(
            src_ref=stage.at[k, strip(m), :], dst_ref=from_end.at[strip(m), :],
            send_sem=carry_send.at[k], recv_sem=end_recv.at[m],
            device_id={"pipe": section + (1 - 2 * k), "tensor": shards - 1 - shard}).start()

    def carry_all(start, stop, k):
        @pl.loop(start, stop)
        def _(m):
            carry(m, k)

    def g_share(m):
        return pltpu.make_async_remote_copy(
            src_ref=g_all.at[held(replica, m), :], dst_ref=g_all.at[held(replica, m), :],
            send_sem=g_send.at[0], recv_sem=share_recv, device_id={"dp": sibling})

    def g_cross(m, o):
        return pltpu.make_async_remote_copy(
            src_ref=g_all.at[held(replica, m), :], dst_ref=g_all.at[held(replica, m), :],
            send_sem=g_send.at[o], recv_sem=g_recv.at[m, o - 1],
            device_id={"dp": 2 * lax.rem(pair + o, pairs) + side})

    def g_pass(m, o):
        source = 2 * lax.rem(pair + pairs - o, pairs) + side
        return pltpu.make_async_remote_copy(
            src_ref=g_all.at[held(source, m), :], dst_ref=g_all.at[held(source, m), :],
            send_sem=pass_send.at[o], recv_sem=pass_recv.at[o], device_id={"dp": sibling})

    def x_share(o):
        return pltpu.make_async_remote_copy(
            src_ref=x_buf.at[o], dst_ref=x_all.at[block(replica), :],
            send_sem=x_send.at[o], recv_sem=x_recv.at[o],
            device_id={"dp": lax.rem(replica + o, replicas)})

    def dequantize():
        s_copy().wait()
        s_buf[...] = jnp.transpose(jnp.broadcast_to(r_buf[...], (128, tok)))

        @pl.loop(0, replicas)
        def _(i):
            o = replicas - 1 - i
            c_copy(o).wait()

            @pl.loop(0, 4)
            def _(m):
                part = pl.ds(pl.multiple_of(m * (tok // 4), tok // 4), tok // 4)
                own = pl.ds(pl.multiple_of(replica * tok + m * (tok // 4), tok // 4), tok // 4)
                value = (c_buf[o, part, :].astype(jnp.float32) * s_buf[part, 0:1]).astype(jnp.bfloat16)

                @pl.when(o > 0)
                def _():
                    x_buf[o, part, :] = value

                @pl.when(o == 0)
                def _():
                    x_all[own, :] = value

            @pl.when(o > 0)
            def _():
                x_share(o).start()

    def launch(m, j):
        straight = j == shards - 1 - shard

        @pl.when(at_end & straight & jnp.logical_not(detoured(m)))
        def _():
            to_end(m).start()

        @pl.when(at_end & straight & detoured(m) & is_last)
        def _():
            to_stage(m, 0).start()

        @pl.when(at_end & straight & detoured(m) & jnp.logical_not(is_last))
        def _():
            to_stage(m, 1).start()

        @pl.when(at_left & (j > 0) & jnp.logical_not(straight))
        def _():
            to_right(m, j).start()

        @pl.when(at_right & (j < shards - 1) & jnp.logical_not(straight))
        def _():
            to_left(m, j).start()

    def launch_next(m):
        @pl.when(shard == 1)
        def _():
            to_right(m, shards - 1).start()

        @pl.when(shard == shards - 2)
        def _():
            to_left(m, 0).start()

    def spread(m):
        g_share(m).start()

        @pl.loop(1, pairs)
        def _(o):
            g_cross(m, o).start()

    def pass_on(m):
        @pl.loop(1, pairs)
        def _(o):
            g_cross(m, o).wait_recv()
            g_pass(m, o).start()

    def w_part(j):
        return w_buf[pl.ds(pl.multiple_of(j * cols, cols), cols), :]

    def produce_all():
        g_load().wait()

        @pl.loop(0, shards)
        def _(i):
            j = order(i)
            w_copy(j).wait()
            prod[j, :, :] = lax.dot_general(
                g_all[block(replica), :], w_part(j), NT, preferred_element_type=jnp.float32
            ).astype(jnp.bfloat16)
            launch(0, j)

            @pl.when(i == 0)
            def _():
                @pl.loop(0, LEAD)
                def _(m):
                    launch_next(m)

        @pl.when(at_end)
        def _():
            @pl.loop(1, MICRO)
            def _(m):
                @pl.loop(0, shards)
                def _(i):
                    launch(m, order(i))

    def produce(m):
        hop(m).wait_recv()
        spread(m)

        @pl.loop(0, shards)
        def _(i):
            j = order(i)
            prod[j, strip(m), :] = lax.dot_general(
                g_all[held(replica, m), :], w_part(j), NT, preferred_element_type=jnp.float32
            ).astype(jnp.bfloat16)
            launch(m, j)

            @pl.when(i == 0)
            def _():
                launch_next(m)

    def add_in(m, j, arrived):
        part = strip(m)
        total = prod[j, part, :].astype(jnp.float32) + arrived[j, part, :].astype(jnp.float32)
        prod[j, part, :] = total.astype(jnp.bfloat16)

    def relay(m, rightward):
        @pl.loop(0, shards - 1)
        def _(i):
            far = shards - 1 - i
            right, left = shard + far, shard - far

            @pl.when(rightward & (shard > 0) & (right < shards) & ((shard > 1) | (right < shards - 1)))
            def _():
                to_right(m, right).wait_recv()
                add_in(m, right, from_left)
                to_right(m, right).start()

            @pl.when(jnp.logical_not(rightward) & (shard < shards - 1) & (left >= 0) & ((shard < shards - 2) | (left > 0)))
            def _():
                to_left(m, left).wait_recv()
                add_in(m, left, from_right)
                to_left(m, left).start()

    def finish(m):
        part = strip(m)

        @pl.when(shard > 0)
        def _():
            to_right(m, shard).wait_recv()

        @pl.when(shard < shards - 1)
        def _():
            to_left(m, shard).wait_recv()

        @pl.when(at_end)
        def _():
            to_end(m).wait_recv()

        def of(ref):
            return ref[shard, part, :].astype(jnp.float32)

        own = of(prod) + g_all[held(replica, m), :].astype(jnp.float32)

        @pl.when(jnp.logical_not(at_end))
        def _():
            grad_in[part, :] = (own + (of(from_left) + of(from_right))).astype(jnp.bfloat16)

        def settle(condition, inner):
            @pl.when(condition)
            def _():
                grad_in[part, :] = (own + (of(inner) + from_end[part, :].astype(jnp.float32))).astype(jnp.bfloat16)

        settle(at_left, from_right)
        settle(at_right, from_left)

        @pl.when(section > 0)
        def _():
            hop(m).start()

    near = 2 * shard < shards
    late = jnp.where(at_end, END_LATE, MID_LATE)

    def relays(m):
        relay(m, near)
        relay(m, jnp.logical_not(near))

    @pl.when(is_last)
    def _():
        produce_all()

        @pl.loop(0, MICRO)
        def _(m):
            @pl.when(jnp.logical_not(at_end))
            def _():
                relays(m)

                @pl.when(m + LEAD < MICRO)
                def _():
                    launch_next(m + LEAD)

            @pl.when(m == 0)
            def _():
                load_codes()

                @pl.loop(0, MICRO)
                def _(n):
                    spread(n)

            @pl.when(at_end)
            def _():
                finish(m)

            @pl.when(jnp.logical_not(at_end))
            def _():
                @pl.when(m < PROMPT)
                def _():
                    finish(m)

                @pl.when(m >= PROMPT + WAIT)
                def _():
                    finish(m - WAIT)

            @pl.when(m == CODES_AT)
            def _():
                dequantize()

        @pl.when(jnp.logical_not(at_end))
        def _():
            @pl.loop(MICRO - WAIT, MICRO)
            def _(m):
                finish(m)

        @pl.loop(0, MICRO)
        def _(m):
            pass_on(m)

    below, above = at_end & (section > 0), at_end & (section == sections - 2)

    @pl.when(jnp.logical_not(is_last))
    def _():
        dequantize()

        @pl.when(above)
        def _():
            carry_all(FILL, FULL, 0)

        @pl.loop(0, shards)
        def _(i):
            w_copy(order(i)).wait()

        behind = jnp.where(at_end, END_LAG, MID_LAG)

        @pl.loop(0, MICRO)
        def _(s):
            def at(lag, action):
                @pl.when(s >= lag)
                def _():
                    action(s - lag)

            produce(s)
            at(NEAR_LAG, lambda m: relay(m, near))
            at(FAR_LAG, lambda m: relay(m, jnp.logical_not(near)))
            at(PASS_LAG, pass_on)
            at(behind, finish)

        @pl.loop(MICRO - NEAR_LAG, MICRO)
        def _(m):
            relay(m, near)

        @pl.loop(MICRO - FAR_LAG, MICRO)
        def _(m):
            relay(m, jnp.logical_not(near))

        @pl.loop(MICRO - PASS_LAG, MICRO)
        def _(m):
            pass_on(m)

        @pl.loop(MICRO - behind, MICRO - late)
        def _(m):
            finish(m)

    @pl.when(below)
    def _():
        carry_all(DRAIN, STOP, 1)

    @pl.loop(1, replicas)
    def _(o):
        x_share(o).wait_recv()

    def sent(source, sem):
        pltpu.make_async_copy(source, source, sem).wait()

    sent(g_all.at[block(sibling), :], share_recv)

    @pl.loop(1, pairs)
    def _(o):
        sent(g_all.at[block(2 * lax.rem(pair + pairs - o, pairs) + 1 - side), :], pass_recv.at[o])

    chunk = rows_a_step(width)

    @pl.loop(0, weight_part.shape[0] // chunk)
    def _(i):
        part = pl.ds(pl.multiple_of(i * chunk, chunk), chunk)
        weight_part[part, :] = lax.dot_general(x_all[:, part], g_all[...], TN, preferred_element_type=jnp.float32)

    @pl.when(jnp.logical_not(is_last))
    def _():
        @pl.loop(MICRO - late, MICRO)
        def _(m):
            finish(m)

    @pl.loop(0, shards)
    def _(j):
        @pl.when((j != shard) & jnp.logical_not(at_end & (j == shards - 1 - shard)))
        def _():
            sent(prod.at[j], sum_send.at[j])

    @pl.when(at_end)
    def _():
        sent(prod.at[shards - 1 - shard], end_send)

    @pl.when(above)
    def _():
        sent(stage.at[0, pl.ds(0, (FULL - FILL) * rows), :], carry_send.at[0])

    @pl.when(below)
    def _():
        sent(stage.at[1, pl.ds(0, (STOP - DRAIN) * rows), :], carry_send.at[1])

    @pl.when(section > 0)
    def _():
        sent(grad_in, hop_send)

    sent(g_all.at[block(replica), :], g_send.at[0])

    @pl.loop(1, pairs)
    def _(o):
        sent(g_all.at[block(replica), :], g_send.at[o])
        sent(g_all.at[block(replica), :], pass_send.at[o])

    @pl.loop(1, replicas)
    def _(o):
        x_share(o).wait_send()


def per_device(weights, codes, scales, grad_out):
    sections, shards, replicas = (lax.axis_size(n) for n in ("pipe", "tensor", "dp"))
    tok, cols = grad_out.shape
    depth = weights.shape[1]
    width = depth // replicas
    pairs = replicas // 2
    low = jnp.bfloat16
    dma = pltpu.SemaphoreType.DMA
    far = pl.BlockSpec(memory_space=pltpu.MemorySpace.HBM)
    inside = pl.BlockSpec(memory_space=pltpu.VMEM)
    chunk = rows_a_step(width)
    done = min(KEPT, width // chunk - 1) * chunk
    later = (width - done) // chunk
    handed = pl.pallas_call(
        functools.partial(relay_kernel, sections=sections, shards=shards, replicas=replicas),
        out_shape=(
            pltpu.VMEM((tok, cols), low),
            pltpu.VMEM((done, cols), jnp.float32),
            pltpu.VMEM((replicas * tok, width), low),
            pltpu.VMEM((replicas * tok, cols), low),
        ),
        in_specs=[far, far, far, far],
        out_specs=(inside,) * 4,
        scratch_shapes=[
            pltpu.VMEM((depth, cols), low),
            pltpu.VMEM((replicas, tok, width), jnp.int32),
            pltpu.VMEM((1, tok), jnp.float32),
            pltpu.VMEM((tok, 128), jnp.float32),
            pltpu.VMEM((replicas, tok, width), low),
            pltpu.VMEM((shards, tok, cols), low),
            pltpu.VMEM((shards, tok, cols), low),
            pltpu.VMEM((shards, tok, cols), low),
            pltpu.VMEM((tok, cols), low),
            pltpu.VMEM((2, tok, cols), low),
            dma((shards,)), dma((replicas,)), dma(()), dma(()), dma(()), dma((MICRO,)),
            dma((shards,)), dma((MICRO, shards + 1)), dma(()), dma((MICRO,)), dma((2, max(FULL - FILL, STOP - DRAIN))), dma((2,)),
            dma((pairs,)), dma(()), dma((MICRO, pairs - 1)), dma((pairs,)), dma((pairs,)),
            dma((replicas,)), dma((replicas,)),
        ],
        compiler_params=pltpu.CompilerParams(collective_id=0, has_side_effects=True, vmem_limit_bytes=57 * 2**20 - 2**18),
    )(weights[0], codes[0], scales, grad_out)
    grad_in, weight_grad = pl.pallas_call(
        closing_kernel,
        out_shape=(
            jax.ShapeDtypeStruct((tok, cols), low),
            jax.ShapeDtypeStruct((width, cols), jnp.float32),
        ),
        in_specs=[inside] * 4,
        out_specs=(far, far),
        scratch_shapes=[pltpu.VMEM((later, chunk, cols), jnp.float32), dma((later,)), dma(()), dma(())],
        compiler_params=pltpu.CompilerParams(vmem_limit_bytes=LIMIT * 2**20),
    )(*handed)
    return grad_in[None], weight_grad[None]


def solution(mesh):
    placed = (P("pipe", None, "tensor"), P("pipe", "dp", None), P("pipe", "dp"), P("dp", "tensor"))
    return jax.shard_map(
        per_device,
        mesh=mesh,
        in_specs=placed,
        out_specs=(P("pipe", "dp", "tensor"), P("pipe", "dp", "tensor")),
        check_vma=False,
    )
```
